32 devices in a mesh: ctx: 16 (over z, y, x), wt: 2 (over core).
Axes of the slice: x: 2, y: 2, z: 4, core: 2. Of those that a mesh axis runs over, the one named last changes fastest.
Arguments:
- layer_input: bfloat16 [2048, 2048], P('ctx'), may hold values from -6 to 6
- block_table: int32 [16, 2], replicated, may hold values from 0 to 31, as said below
- routes: int32 [2048, 6], P('ctx'), may hold values from 0 to 15, all different within a row; in each aligned block of 128 rows (0 to 127, 128 to 255, ...) at most 64 rows name the same one
- grad_output: bfloat16 [2048, 2048], P('ctx'), may hold values from -6 to 6
- norm1_gain: bfloat16 [2048], P('ctx'), may hold values from 0.5 to 1.5
- query_down_weight: bfloat16 [2048, 1536], P('ctx'), may hold values from -0.125 to 0.125
- q_gain: bfloat16 [1536], P('ctx'), may hold values from 0.5 to 1.5
- q_up: bfloat16 [1536, 3072], P('ctx', 'wt'), may hold values from -0.15625 to 0.15625
- kv_down: bfloat16 [2048, 576], P('ctx'), may hold values from -0.125 to 0.125
- kv_gain: bfloat16 [512], P('ctx'), may hold values from 0.5 to 1.5
- kv_up: bfloat16 [512, 4096], P('ctx', 'wt'), may hold values from -0.25 to 0.25
- out_proj: bfloat16 [2048, 2048], P('ctx', 'wt'), may hold values from -0.375 to 0.375
- norm2_gain: bfloat16 [2048], P('ctx'), may hold values from 0.5 to 1.5
- router: bfloat16 [2048, 16], P('ctx'), may hold values from -0.125 to 0.125
- shared_gate: bfloat16 [2048, 2816], P('ctx', 'wt'), may hold values from -0.125 to 0.125
- shared_up: bfloat16 [2048, 2816], P('ctx', 'wt'), may hold values from -0.125 to 0.125
- shared_down: bfloat16 [2048, 2816], P('ctx', 'wt'), may hold values from -0.109375 to 0.109375
- expert_gate: bfloat16 [16, 2048, 1408], P('ctx', None, 'wt'), may hold values from -0.125 to 0.125
- routed_expert_up_weight: bfloat16 [16, 2048, 1408], P('ctx', None, 'wt'), may hold values from -0.125 to 0.125
- expert_down: bfloat16 [16, 1408, 2048], P('ctx', 'wt'), may hold values from -0.15625 to 0.15625
Outputs:
- output: bfloat16 [2048, 2048], P('ctx')
- grad_input: float32 [2048, 2048], P('ctx')
- grad_norm1_gain: float32 [2048], P('ctx')
- grad_query_down_weight: float32 [2048, 1536], P('ctx')
- grad_q_gain: float32 [1536], P('ctx')
- grad_q_up: float32 [1536, 3072], P('ctx', 'wt')
- grad_kv_down: float32 [2048, 576], P('ctx')
- grad_kv_gain: float32 [512], P('ctx')
- grad_kv_up: float32 [512, 4096], P('ctx', 'wt')
- grad_out_proj: float32 [2048, 2048], P('ctx', 'wt')
- grad_norm2_gain: float32 [2048], P('ctx')
- grad_router: float32 [2048, 16], P('ctx')
- grad_shared_gate: float32 [2048, 2816], P('ctx', 'wt')
- grad_shared_up: float32 [2048, 2816], P('ctx', 'wt')
- grad_shared_down: float32 [2048, 2816], P('ctx', 'wt')
- grad_expert_gate: float32 [16, 2048, 1408], P('ctx', None, 'wt')
- grad_expert_up: float32 [16, 2048, 1408], P('ctx', None, 'wt')
- grad_expert_down: float32 [16, 1408, 2048], P('ctx', 'wt')
The draws below stay inside these ranges and needn't reach their ends.
Inputs may be any that keep to these rules, and one draw needn't show every extreme that they name: `block_table`: row i holds (b, 31 - b), and every b of 0 to 15 stands in exactly one row. `routes`: each row names 6 different experts. In the rows of one device (aligned blocks of 128 rows) no expert is named by more than 64 rows, and in some block one expert is named by exactly 64.
All inputs are finite; a program needn't handle non-finite values.
Results may differ from the reference program's by a relative error of at most 0.02.
Values may be sent and summed in bfloat16 or wider, within the bound.
No kernel may reach another device: no remote copies, remote signals or barrier semaphores. Data moves between devices by JAX's collectives and lax.ppermute only.
A program may use at most 384 MiB of HBM per device.

```python
import math
import jax
import jax.numpy as jnp
import numpy as np
from jax import lax

D = 2048
HEADS = 16
NOPE = 128
ROPE = 64
VDIM = 128
QR = 1536
KVR = 512
EXPERT_FF = 1408
SHARED_FF = 2816
TOPK = 6
BLOCK = 64
EXPERTS = 16
T_DEV = 128
LENGTH = 2048
MOST = 64
N_CTX = 16


def draw_block_table(key, part):
    pair_count = LENGTH // (2 * BLOCK)
    order = jax.random.permutation(key, pair_count).astype(jnp.int32)
    return jnp.stack([order, 2 * pair_count - 1 - order], axis=1).astype(jnp.int32)


def levels(rng, dims, cuts, low, high):
    def one(dim, blocks):
        heights = jax.random.uniform(jax.random.fold_in(jax.random.fold_in(rng, 6), dim), (blocks,), jnp.float32, low / len(cuts), high / len(cuts))
        return jnp.repeat(jnp.exp(heights), dims[dim] // blocks).reshape((-1,) + (1,) * (len(dims) - dim - 1))

    level = one(*cuts[0])
    for cut in cuts[1:]:
        level = level * one(*cut)
    return level


def deal_out(own_key, own, number, rows, amount, top, reach, lean):
    sequence = jax.random.permutation(own_key, amount)
    heavy_load, common = shares(amount, rows * top, reach, lean, True), shares(amount, rows * top, reach, lean, False)
    places = jnp.arange(amount)

    def named(sizes, turn):
        used = int((sizes > 0).sum())
        fixed = max(1, used // 4)
        passed = fixed + (places - fixed + turn * (used - fixed)) % max(1, amount - fixed)
        return jnp.zeros((amount,), jnp.int32).at[sequence[jnp.where(places < fixed, places, passed)]].set(jnp.asarray(sizes, jnp.int32))

    sizes = jnp.where(number % 4 == 0, named(heavy_load, number // 4), named(common, number - number // 4 - 1))
    mixed = jax.random.permutation(jax.random.fold_in(own, 3), amount)
    donor, receiver = mixed[0:amount // 2 * 2:2], mixed[1:amount // 2 * 2:2]
    room = jnp.minimum(sizes[donor] - 1, reach - sizes[receiver]) // 2
    room = jnp.where((donor == sequence[0]) | (receiver == sequence[0]) | (sizes[receiver] == 0), 0, jnp.maximum(room, 0))
    passed = jax.random.randint(jax.random.fold_in(own, 4), (amount // 2,), 0, 1 << 20) % (room + 1)
    sizes = sizes.at[donor].add(-passed).at[receiver].add(passed)
    labels = jnp.searchsorted(jnp.cumsum(sizes), jnp.arange(rows * top), side="right").astype(jnp.int32)
    table = labels.reshape(top, rows).T
    table = table[jax.random.permutation(jax.random.fold_in(own, 1), rows)]
    turn = jax.random.randint(jax.random.fold_in(own, 2), (rows, 1), 0, top)
    return jnp.take_along_axis(table, (jnp.arange(top)[None, :] + turn) % top, axis=1)


def shares(number_of, total, most, lean, full):
    loads = [(1 << 20) // math.isqrt(rank ** lean) + 1 for rank in range(1, number_of + 1)]
    largest = most if full else min(most, max(-(-total // number_of), total * loads[0] // sum(loads)))
    least = 1 if total - largest >= number_of - 1 else 0
    holding, spare = [largest] + [least] * (number_of - 1), total - largest - least * (number_of - 1)
    while spare > 0:
        movable = [i for i in range(1, number_of) if holding[i] < largest] or [i for i in range(1, number_of) if holding[i] < most]
        whole, remaining = sum([loads[i] for i in movable]), spare
        for i in movable:
            addition = min(most - holding[i], max(1, remaining * loads[i] // whole), spare)
            holding[i] = holding[i] + addition
            spare = spare - addition
    return np.array(holding)


def normal_values(key, extent, spread, limit, split=(), held_as=jnp.bfloat16):
    gain = levels(key, extent, split, -0.22, 0.18) if split else 1.0
    entries = jax.random.normal(key, extent, jnp.float32) * spread * gain
    return jnp.minimum(jnp.maximum(entries, -limit), limit).astype(held_as)


def setup_inputs(seed: int = 0) -> dict:
    arg_keys = jax.random.split(jax.random.key(seed), 21)
    layer_input = normal_values(arg_keys[0], (LENGTH, D), 1.0, 6.0, ((0, 16),))
    block_table = draw_block_table(jax.random.fold_in(arg_keys[20], 71), 0)
    routes_keys = jax.random.split(jax.random.fold_in(arg_keys[2], 1), LENGTH // T_DEV)
    routes_turns = jax.random.permutation(jax.random.fold_in(arg_keys[2], 3), LENGTH // T_DEV)
    routes = jax.vmap(lambda own, number: deal_out(jax.random.fold_in(arg_keys[2], 2), own, number, T_DEV, EXPERTS, TOPK, MOST, 1))(routes_keys, routes_turns).reshape((LENGTH, TOPK))
    grad_output = normal_values(arg_keys[3], (LENGTH, D), 1.0, 6.0, ((0, 16),))
    norm1_gain = jnp.clip(1.0 + 0.1 * jax.random.normal(arg_keys[4], (D,), jnp.float32), 0.5, 1.5).astype(jnp.bfloat16)
    query_down_weight = normal_values(arg_keys[5], (D, QR), D ** -0.5, 0.125, ((0, 16),))
    q_gain = jnp.clip(1.0 + 0.1 * jax.random.normal(arg_keys[6], (QR,), jnp.float32), 0.5, 1.5).astype(jnp.bfloat16)
    q_up = normal_values(arg_keys[7], (QR, HEADS * (NOPE + ROPE)), QR ** -0.5, 0.15625, ((0, 16), (1, 2)))
    kv_down = normal_values(arg_keys[8], (D, KVR + ROPE), D ** -0.5, 0.125, ((0, 16),))
    kv_gain = jnp.clip(1.0 + 0.1 * jax.random.normal(arg_keys[9], (KVR,), jnp.float32), 0.5, 1.5).astype(jnp.bfloat16)
    kv_up = normal_values(arg_keys[10], (KVR, HEADS * (NOPE + VDIM)), KVR ** -0.5, 0.25, ((0, 16), (1, 2)))
    out_proj = normal_values(arg_keys[11], (D, HEADS * VDIM), (HEADS * VDIM // 8) ** -0.5, 0.375, ((0, 16), (1, 2)))
    norm2_gain = jnp.clip(1.0 + 0.1 * jax.random.normal(arg_keys[12], (D,), jnp.float32), 0.5, 1.5).astype(jnp.bfloat16)
    router = normal_values(arg_keys[13], (D, EXPERTS), D ** -0.5, 0.125, ((0, 16),))
    shared_gate = normal_values(arg_keys[14], (D, SHARED_FF), D ** -0.5, 0.125, ((0, 16), (1, 2)))
    shared_up = normal_values(arg_keys[15], (D, SHARED_FF), D ** -0.5, 0.125, ((0, 16), (1, 2)))
    shared_down = normal_values(arg_keys[16], (D, SHARED_FF), SHARED_FF ** -0.5, 0.109375, ((0, 16), (1, 2)))
    expert_gate = normal_values(arg_keys[17], (EXPERTS, D, EXPERT_FF), D ** -0.5, 0.125, ((0, 16), (2, 2)))
    routed_expert_up_weight = normal_values(arg_keys[18], (EXPERTS, D, EXPERT_FF), D ** -0.5, 0.125, ((0, 16), (2, 2)))
    expert_down = normal_values(arg_keys[19], (EXPERTS, EXPERT_FF, D), EXPERT_FF ** -0.5, 0.15625, ((0, 16), (1, 2)))
    return {"layer_input": layer_input, "block_table": block_table, "routes": routes, "grad_output": grad_output, "norm1_gain": norm1_gain, "query_down_weight": query_down_weight, "q_gain": q_gain, "q_up": q_up, "kv_down": kv_down, "kv_gain": kv_gain, "kv_up": kv_up, "out_proj": out_proj, "norm2_gain": norm2_gain, "router": router, "shared_gate": shared_gate, "shared_up": shared_up, "shared_down": shared_down, "expert_gate": expert_gate, "routed_expert_up_weight": routed_expert_up_weight, "expert_down": expert_down}


rms_epsilon = 1e-06
rope_base = 50000.0
route_scale = 2.446
highest = lax.Precision.HIGHEST

def to_half(values):
    return lax.optimization_barrier(values.astype(jnp.bfloat16))

def dot_rows(left_mat, right_mat):
    return lax.dot_general(left_mat, right_mat, (((1,), (1,)), ((), ())), preferred_element_type=jnp.float32)

def dot_cols(left_mat, right_mat):
    return lax.dot_general(left_mat, right_mat, (((0,), (0,)), ((), ())), preferred_element_type=jnp.float32)

def normalize(values, weights):
    inverse = lax.rsqrt(lax.optimization_barrier(jnp.mean(values * values, axis=-1, keepdims=True)) + rms_epsilon)
    return (values * inverse * weights, inverse)

def norm_backward(upstream, values, inverse, weights):
    unit_rows = values * inverse
    scaled = upstream * weights
    inner_mean = lax.optimization_barrier(jnp.mean(scaled * unit_rows, axis=-1, keepdims=True))
    return (inverse * (scaled - unit_rows * inner_mean), lax.optimization_barrier(jnp.sum(upstream * unit_rows, axis=0)))

def rope_tables(positions):
    half_dim = ROPE // 2
    exponent = jnp.arange(half_dim, dtype=jnp.float32) * (2.0 / ROPE)
    frequency = jnp.exp(-exponent * math.log(rope_base))
    angles = positions.astype(jnp.float32)[:, None] * frequency[None, :]
    return (jnp.cos(angles), jnp.sin(angles))

def rotate(values, cosine, sine_part):
    half_dim = values.shape[-1] // 2
    first_half = values[..., :half_dim]
    second_half = values[..., half_dim:]
    return jnp.concatenate([first_half * cosine - second_half * sine_part, first_half * sine_part + second_half * cosine], axis=-1)

def unrotate(values, cosine, sine_part):
    half_dim = values.shape[-1] // 2
    first_half = values[..., :half_dim]
    second_half = values[..., half_dim:]
    return jnp.concatenate([first_half * cosine + second_half * sine_part, second_half * cosine - first_half * sine_part], axis=-1)

def silu_parts(values):
    sigma = jax.nn.sigmoid(values)
    return (values * sigma, sigma * (1.0 + values * (1.0 - sigma)))

def reference(layer_input, block_table, routes, grad_output, norm1_gain, query_down_weight, q_gain, q_up, kv_down, kv_gain, kv_up, out_proj, norm2_gain, router, shared_gate, shared_up, shared_down, expert_gate, routed_expert_up_weight, expert_down):
    length_all = layer_input.shape[0]
    offsets = jnp.arange(BLOCK, dtype=jnp.int32)
    positions = (block_table[:, :, None] * BLOCK + offsets[None, None, :]).reshape(-1).astype(jnp.int32)
    cosine, sine_part = rope_tables(positions)
    score_scale = (NOPE + ROPE) ** (-0.5)
    inputs = layer_input.astype(jnp.float32)
    normed_f, inverse_one = normalize(inputs, norm1_gain.astype(jnp.float32))
    normed = to_half(normed_f)
    q_latent = jnp.dot(normed, query_down_weight, preferred_element_type=jnp.float32)
    q_norm_f, q_inverse = normalize(q_latent, q_gain.astype(jnp.float32))
    q_normed = to_half(q_norm_f)
    kv_latent = jnp.dot(normed, kv_down, preferred_element_type=jnp.float32)
    latent_f, kv_inverse = normalize(kv_latent[:, :KVR], kv_gain.astype(jnp.float32))
    latent = to_half(latent_f)
    key_rope = to_half(rotate(kv_latent[:, KVR:], cosine, sine_part))
    query_full = jnp.dot(q_normed, q_up, preferred_element_type=jnp.float32).reshape(length_all, HEADS, NOPE + ROPE)
    queries = to_half(jnp.concatenate([query_full[..., :NOPE], rotate(query_full[..., NOPE:], cosine[:, None, :], sine_part[:, None, :])], axis=-1))
    key_values = to_half(jnp.dot(latent, kv_up, preferred_element_type=jnp.float32)).reshape(length_all, HEADS, NOPE + VDIM)
    key_nope_f = key_values[..., :NOPE].astype(jnp.float32)
    values_f = key_values[..., NOPE:].astype(jnp.float32)
    key_rope_f = key_rope.astype(jnp.float32)
    query_block = min(512, length_all)
    block_count = length_all // query_block

    def block_scores(query_blk, position_blk):
        query_f = query_blk.astype(jnp.float32)
        scores = jnp.einsum('thd,lhd->htl', query_f[..., :NOPE], key_nope_f, precision=highest)
        scores = scores + jnp.einsum('thr,lr->htl', query_f[..., NOPE:], key_rope_f, precision=highest)
        allowed = position_blk[:, None] >= positions[None, :]
        return (scores * score_scale, allowed)

    def attend_forward(operands):
        query_blk, position_blk = operands
        scores, allowed = block_scores(query_blk, position_blk)
        raw_weights = jnp.where(allowed[None], jnp.exp(scores), 0.0)
        log_total = jnp.log(lax.optimization_barrier(jnp.sum(raw_weights, axis=-1)))
        probability = to_half(jnp.where(allowed[None], jnp.exp(scores - log_total[..., None]), 0.0))
        result = jnp.einsum('htl,lhv->thv', probability.astype(jnp.float32), values_f, precision=highest)
        return (to_half(result), log_total)
    query_blocks = queries.reshape(block_count, query_block, HEADS, NOPE + ROPE)
    position_blocks = positions.reshape(block_count, query_block)
    attention_blocks, log_blocks = lax.map(attend_forward, (query_blocks, position_blocks))
    attention = attention_blocks.reshape(length_all, HEADS * VDIM)
    hidden_one = inputs + dot_rows(attention, out_proj)
    normed2_f, inverse_two = normalize(hidden_one, norm2_gain.astype(jnp.float32))
    normed_two = to_half(normed2_f)
    logits = jnp.dot(normed_two, router, preferred_element_type=jnp.float32)
    sigma = jax.nn.sigmoid(logits)
    picked = routes[..., None] == jnp.arange(EXPERTS, dtype=jnp.int32)[None, None, :]
    chosen = lax.optimization_barrier(jnp.sum(jnp.where(picked, sigma[:, None, :], 0.0), axis=-1))
    chosen_total = lax.optimization_barrier(jnp.sum(chosen, axis=-1, keepdims=True))
    gates = route_scale * chosen / chosen_total
    block_routes = routes.reshape(N_CTX, T_DEV * TOPK)
    one_hot = (block_routes[..., None] == jnp.arange(EXPERTS, dtype=jnp.int32)[None, None, :]).astype(jnp.int32)
    slots = lax.optimization_barrier(jnp.sum((jnp.cumsum(one_hot, axis=1) - 1) * one_hot, axis=-1))
    device_ids = jnp.arange(N_CTX, dtype=jnp.int32)[:, None]
    per_expert = N_CTX * MOST
    targets = (block_routes * per_expert + device_ids * MOST + slots).reshape(-1).astype(jnp.int32)
    send_rows = jnp.zeros((EXPERTS * per_expert, D), jnp.bfloat16).at[targets].set(jnp.repeat(normed_two, TOPK, axis=0))
    expert_rows = send_rows.reshape(EXPERTS, per_expert, D)

    def expert_forward(operands):
        rows_in, gate_mat, up_mat, down_mat = operands
        gate_before_silu = jnp.dot(rows_in, gate_mat, preferred_element_type=jnp.float32)
        up_pre = jnp.dot(rows_in, up_mat, preferred_element_type=jnp.float32)
        silu_activated_rows, slope = silu_parts(gate_before_silu)
        hidden = to_half(silu_activated_rows * up_pre)
        return jnp.dot(hidden, down_mat, preferred_element_type=jnp.float32)
    expert_out = lax.map(expert_forward, (expert_rows, expert_gate, routed_expert_up_weight, expert_down))
    picked_out = expert_out.reshape(-1, D)[targets].reshape(length_all, TOPK, D)
    routed = lax.optimization_barrier(jnp.sum(gates[..., None] * picked_out, axis=1))
    shared_gate_pre = jnp.dot(normed_two, shared_gate, preferred_element_type=jnp.float32)
    shared_up_pre = jnp.dot(normed_two, shared_up, preferred_element_type=jnp.float32)
    shared_act, shared_slope = silu_parts(shared_gate_pre)
    shared_hidden = to_half(shared_act * shared_up_pre)
    shared_out = dot_rows(shared_hidden, shared_down)
    output = (hidden_one + routed + shared_out).astype(jnp.bfloat16)
    upstream = grad_output.astype(jnp.float32)
    shared_back = jnp.dot(grad_output, shared_down, preferred_element_type=jnp.float32)
    grad_shared_gate_pre = to_half(shared_back * shared_up_pre * shared_slope)
    grad_shared_up_pre = to_half(shared_back * shared_act)
    grad_shared_down = dot_cols(grad_output, shared_hidden)
    grad_shared_gate = dot_cols(normed_two, grad_shared_gate_pre)
    grad_shared_up = dot_cols(normed_two, grad_shared_up_pre)
    grad_normed_two = dot_rows(grad_shared_gate_pre, shared_gate) + dot_rows(grad_shared_up_pre, shared_up)
    grad_gates = lax.optimization_barrier(jnp.sum(upstream[:, None, :] * picked_out, axis=-1))
    back_rows = to_half(gates[..., None] * upstream[:, None, :]).reshape(-1, D)
    back_buffer = jnp.zeros((EXPERTS * per_expert, D), jnp.bfloat16).at[targets].set(back_rows).reshape(EXPERTS, per_expert, D)

    def expert_backward(operands):
        rows_in, rows_back, gate_mat, up_mat, down_mat = operands
        gate_before_silu = jnp.dot(rows_in, gate_mat, preferred_element_type=jnp.float32)
        up_pre = jnp.dot(rows_in, up_mat, preferred_element_type=jnp.float32)
        silu_activated_rows, slope = silu_parts(gate_before_silu)
        hidden = to_half(silu_activated_rows * up_pre)
        returned_hidden_rows = dot_rows(rows_back, down_mat)
        gate_grad = to_half(returned_hidden_rows * up_pre * slope)
        up_grad = to_half(returned_hidden_rows * silu_activated_rows)
        rows_grad = dot_rows(gate_grad, gate_mat) + dot_rows(up_grad, up_mat)
        return (rows_grad, dot_cols(rows_in, gate_grad), dot_cols(rows_in, up_grad), dot_cols(hidden, rows_back))
    rows_grad, grad_expert_gate, grad_expert_up, grad_expert_down = lax.map(expert_backward, (expert_rows, back_buffer, expert_gate, routed_expert_up_weight, expert_down))
    grad_normed_two = grad_normed_two + lax.optimization_barrier(jnp.sum(rows_grad.reshape(-1, D)[targets].reshape(length_all, TOPK, D), axis=1))
    grad_chosen = (route_scale * grad_gates - lax.optimization_barrier(jnp.sum(grad_gates * gates, axis=-1, keepdims=True))) / chosen_total
    grad_logit_pick = grad_chosen * chosen * (1.0 - chosen)
    grad_logits = to_half(lax.optimization_barrier(jnp.sum(jnp.where(picked, grad_logit_pick[..., None], 0.0), axis=1)))
    grad_normed_two = grad_normed_two + dot_rows(grad_logits, router)
    grad_router = dot_cols(normed_two, grad_logits)
    grad_hidden, grad_norm2_gain = norm_backward(grad_normed_two, hidden_one, inverse_two, norm2_gain.astype(jnp.float32))
    grad_hidden = grad_hidden + upstream
    grad_hidden_half = to_half(grad_hidden)
    grad_out_proj = dot_cols(grad_hidden_half, attention)
    grad_attention = to_half(jnp.dot(grad_hidden_half, out_proj, preferred_element_type=jnp.float32)).reshape(length_all, HEADS, VDIM)

    def attend_backward(carry, operands):
        grad_keys, grad_values, grad_rope = carry
        query_blk, position_blk, attention_blk, grad_blk, log_blk = operands
        scores, allowed = block_scores(query_blk, position_blk)
        exact = jnp.where(allowed[None], jnp.exp(scores - log_blk[..., None]), 0.0)
        probability = to_half(exact).astype(jnp.float32)
        grad_blk_f = grad_blk.astype(jnp.float32)
        delta = jnp.einsum('thv,thv->ht', grad_blk_f, attention_blk.astype(jnp.float32), precision=highest)
        grad_probs = jnp.einsum('thv,lhv->htl', grad_blk_f, values_f, precision=highest)
        grad_scores = to_half(exact * (grad_probs - delta[..., None])).astype(jnp.float32)
        query_f = query_blk.astype(jnp.float32)
        grad_query = score_scale * jnp.concatenate([jnp.einsum('htl,lhd->thd', grad_scores, key_nope_f, precision=highest), jnp.einsum('htl,lr->thr', grad_scores, key_rope_f, precision=highest)], axis=-1)
        grad_keys = grad_keys + score_scale * jnp.einsum('htl,thd->lhd', grad_scores, query_f[..., :NOPE], precision=highest)
        grad_rope = grad_rope + score_scale * jnp.einsum('htl,thr->lr', grad_scores, query_f[..., NOPE:], precision=highest)
        grad_values = grad_values + jnp.einsum('htl,thv->lhv', probability, grad_blk_f, precision=highest)
        return ((grad_keys, grad_values, grad_rope), grad_query)
    start_carry = (jnp.zeros((length_all, HEADS, NOPE), jnp.float32), jnp.zeros((length_all, HEADS, VDIM), jnp.float32), jnp.zeros((length_all, ROPE), jnp.float32))
    attention_heads = attention_blocks
    grad_blocks = grad_attention.reshape(block_count, query_block, HEADS, VDIM)
    (grad_keys, grad_values, grad_rope), grad_query_blocks = lax.scan(attend_backward, start_carry, (query_blocks, position_blocks, attention_heads, grad_blocks, log_blocks))
    grad_queries = grad_query_blocks.reshape(length_all, HEADS, NOPE + ROPE)
    grad_key_values = to_half(jnp.concatenate([grad_keys, grad_values], axis=-1).reshape(length_all, -1))
    grad_kv_up = dot_cols(latent, grad_key_values)
    grad_latent = dot_rows(grad_key_values, kv_up)
    grad_q_rope = unrotate(grad_queries[..., NOPE:], cosine[:, None, :], sine_part[:, None, :])
    grad_query_half = to_half(jnp.concatenate([grad_queries[..., :NOPE], grad_q_rope], axis=-1).reshape(length_all, -1))
    grad_q_up = dot_cols(q_normed, grad_query_half)
    grad_q_normed = dot_rows(grad_query_half, q_up)
    grad_q_latent, grad_q_gain = norm_backward(grad_q_normed, q_latent, q_inverse, q_gain.astype(jnp.float32))
    grad_kv_part, grad_kv_gain = norm_backward(grad_latent, kv_latent[:, :KVR], kv_inverse, kv_gain.astype(jnp.float32))
    grad_rope_raw = unrotate(grad_rope, cosine, sine_part)
    grad_q_latent_half = to_half(grad_q_latent)
    grad_kv_latent_half = to_half(jnp.concatenate([grad_kv_part, grad_rope_raw], axis=-1))
    grad_query_down_weight = dot_cols(normed, grad_q_latent_half)
    grad_kv_down = dot_cols(normed, grad_kv_latent_half)
    grad_normed = dot_rows(grad_q_latent_half, query_down_weight) + dot_rows(grad_kv_latent_half, kv_down)
    grad_input, grad_norm1_gain = norm_backward(grad_normed, inputs, inverse_one, norm1_gain.astype(jnp.float32))
    grad_input = grad_input + grad_hidden
    return (output, grad_input, grad_norm1_gain, grad_query_down_weight, grad_q_gain, grad_q_up, grad_kv_down, grad_kv_gain, grad_kv_up, grad_out_proj, grad_norm2_gain, grad_router, grad_shared_gate, grad_shared_up, grad_shared_down, grad_expert_gate, grad_expert_up, grad_expert_down)
```

```python
import math

import jax
import jax.numpy as jnp
from jax import lax
from jax.experimental import pallas as pl
from jax.experimental.pallas import tpu as pltpu
from jax.sharding import PartitionSpec as P

NOPE = 128
ROPE = 64
VDIM = 128
BLOCK = 64

rms_epsilon = 1e-06
rope_base = 50000.0
route_scale = 2.446


F32 = jnp.float32
BF16 = jnp.bfloat16


def dot(left_mat, right_mat):
    return lax.dot_general(
        left_mat, right_mat, (((1,), (0,)), ((), ())), preferred_element_type=F32
    )


def dot_rows(left_mat, right_mat):
    return lax.dot_general(
        left_mat, right_mat, (((1,), (1,)), ((), ())), preferred_element_type=F32
    )


def dot_cols(left_mat, right_mat):
    return lax.dot_general(
        left_mat, right_mat, (((0,), (0,)), ((), ())), preferred_element_type=F32
    )


def normalize(values, weights):
    inverse = lax.rsqrt(jnp.mean(values * values, axis=-1, keepdims=True) + rms_epsilon)
    return (values * inverse * weights, inverse)


def norm_backward(upstream, values, inverse, weights):
    unit_rows = values * inverse
    scaled = upstream * weights
    inner_mean = jnp.mean(scaled * unit_rows, axis=-1, keepdims=True)
    return (inverse * (scaled - unit_rows * inner_mean), jnp.sum(upstream * unit_rows, axis=0))


def rope_tables(positions):
    half_dim = ROPE // 2
    exponent = jnp.arange(half_dim, dtype=F32) * (2.0 / ROPE)
    frequency = jnp.exp(-exponent * math.log(rope_base))
    angles = positions.astype(F32)[:, None] * frequency[None, :]
    return (jnp.cos(angles), jnp.sin(angles))


def rotate(values, cosine, sine_part):
    half_dim = values.shape[-1] // 2
    first_half = values[..., :half_dim]
    second_half = values[..., half_dim:]
    return jnp.concatenate(
        [
            first_half * cosine - second_half * sine_part,
            first_half * sine_part + second_half * cosine,
        ],
        axis=-1,
    )


def unrotate(values, cosine, sine_part):
    return rotate(values, cosine, -sine_part)


def silu_parts(values):
    sigma = jax.nn.sigmoid(values)
    return (values * sigma, sigma * (1.0 + values * (1.0 - sigma)))


def positions_of(table_rows):
    offsets = jnp.arange(BLOCK, dtype=jnp.int32)
    return (table_rows[:, :, None] * BLOCK + offsets[None, None, :]).reshape(-1)


def exchange(blocks):
    return lax.all_to_all(blocks, "ctx", split_axis=0, concat_axis=0, tiled=True)


def wt_sum(values):
    size = lax.axis_size("wt")
    total = values
    for step in range(1, size):
        total = total + lax.ppermute(values, "wt", [(i, (i + step) % size) for i in range(size)])
    return total


def ring_of(n):
    pairs = n // 2
    return list(range(0, pairs, 2)) + list(range(1, pairs, 2))[::-1]


def hop(values, n, step):
    ring = ring_of(n)
    size = len(ring)
    moves = [
        (2 * ring[i] + x, 2 * ring[(i + step) % size] + x) for i in range(size) for x in range(2)
    ]
    return lax.ppermute(values, "ctx", moves)


def swap(values, n):
    return lax.ppermute(values, "ctx", [(i, i ^ 1) for i in range(n)])


def other_wt(values):
    return lax.ppermute(values, "wt", [(0, 1), (1, 0)])


def chunk_offsets(n):
    pairs = n // 2
    offsets = [0]
    for k in range(1, pairs // 2):
        offsets += [-k, k]
    return offsets + [pairs // 2]


def ring_sum(values, n, w, place, work):
    pairs = n // 2
    q = values.shape[0] // n // 4
    member = place[pairs]
    results = []

    def beside(carried):
        if len(results) < len(work):
            carried, result = lax.optimization_barrier((carried, work[len(results)]()))
            results.append(result)
        return carried

    split = values.reshape(pairs, 2, 2, 2 * q, values.shape[1])
    theirs = other_wt(lax.dynamic_index_in_dim(split, 1 - w, 2, keepdims=False))
    mine = lax.dynamic_index_in_dim(split, w, 2, keepdims=False)
    theirs = beside(theirs)

    def piece(j, x):
        start = (place[j], x, 0, 0)
        size = (1, 1, 2 * q, values.shape[1])
        first = lax.dynamic_slice(mine, start, size).astype(F32)
        return (first + lax.dynamic_slice(theirs, start, size).astype(F32))[0, 0]

    kept = [None] * pairs
    for j in reversed(range(pairs)):
        own, other = piece(j, member), piece(j, 1 - member)
        second = own[q:] + swap(other[q:].astype(BF16), n).astype(F32)
        kept[j] = jnp.concatenate([own[:q], other[:q], second], axis=0)
    cut = 3 * q // 2
    far = kept[-1].astype(BF16)
    none = jnp.zeros_like(kept[0])
    up = none.at[cut:].set(hop(far[cut:], n, 1).astype(F32))
    down = none.at[:cut].set(hop(far[:cut], n, -1).astype(F32))
    up, down = beside((up, down))
    for k in range(pairs // 2 - 1, 0, -1):
        down = hop((kept[2 * k - 1] + down).astype(BF16), n, -1).astype(F32)
        up = hop((kept[2 * k] + up).astype(BF16), n, 1).astype(F32)
        up, down = beside((up, down))
    total = kept[0] + up + down
    first = total[:q] + swap(total[q : 2 * q].astype(BF16), n).astype(F32)
    while len(results) < len(work):
        total = beside(total)
    return jnp.concatenate([first, total[2 * q :]], axis=0), results


def body(
    layer_input,
    block_table,
    routes,
    grad_output,
    norm1_gain,
    query_down_weight,
    q_gain,
    q_up,
    kv_down,
    kv_gain,
    kv_up,
    out_proj,
    norm2_gain,
    router,
    shared_gate,
    shared_up,
    shared_down,
    expert_gate,
    routed_expert_up_weight,
    expert_down,
):
    n = lax.axis_size("ctx")
    wt = lax.axis_size("wt")
    c = lax.axis_index("ctx")
    w = lax.axis_index("wt")
    rows, width = layer_input.shape
    tokens = n * rows
    kvr = kv_gain.shape[0] * n
    qr = q_gain.shape[0] * n
    head_dim = NOPE + ROPE
    heads = q_up.shape[1] // head_dim
    group = math.gcd(4, math.gcd(n, heads))
    groups = n // group
    own_heads = heads // group
    g = c % group
    experts = router.shape[1]
    own_d = norm1_gain.shape[0]
    own_q = q_gain.shape[0]
    latents = qr + kvr + ROPE
    score_scale = head_dim ** (-0.5)
    pairs = n // 2
    ring = ring_of(n)
    spot = jnp.array([ring.index(i) for i in range(pairs)], jnp.int32)[c // 2]
    offsets = jnp.array(chunk_offsets(n), jnp.int32)
    place = jnp.concatenate([jnp.array(ring, jnp.int32)[(spot + offsets) % pairs], (c % 2)[None]])

    def half_rows(values):
        size = values.shape[0] // wt
        return lax.dynamic_slice_in_dim(values, w * size, size, 0)

    def gather_rows(values):
        return lax.all_gather(half_rows(values), ("ctx", "wt"), axis=0, tiled=True)

    def both_halves(mine, axis):
        theirs = other_wt(mine)
        first, second = jnp.where(w == 0, mine, theirs), jnp.where(w == 0, theirs, mine)
        return jnp.concatenate([first, second], axis=axis)

    def group_moves(k):
        return [(i, i ^ k) for i in range(n)]

    def group_sum(values):
        cols = values.shape[1] // 2
        sent = lax.dynamic_slice_in_dim(values, (1 - w) * cols, cols, 1).astype(BF16)
        total = lax.dynamic_slice_in_dim(values, w * cols, cols, 1)
        total = (total + other_wt(sent).astype(F32)).reshape(group, rows, cols)
        own = lax.dynamic_index_in_dim(total, g, 0, keepdims=False)
        for k in range(1, group):
            block = lax.dynamic_index_in_dim(total, g ^ k, 0, keepdims=False).astype(BF16)
            own = own + lax.ppermute(block, "ctx", group_moves(k)).astype(F32)
        return both_halves(own, 1)

    def group_gather(values):
        cols = values.shape[1] // 2
        mine = lax.dynamic_slice_in_dim(values, w * cols, cols, 1)
        out = jnp.zeros((group, rows, cols), values.dtype)
        out = lax.dynamic_update_index_in_dim(out, mine, g, 0)
        for k in range(1, group):
            got = lax.ppermute(mine, "ctx", group_moves(k))
            out = lax.dynamic_update_index_in_dim(out, got, g ^ k, 0)
        return both_halves(out.reshape(group * rows, cols), 1)

    def own_group(values):
        return lax.dynamic_slice_in_dim(values, (c // group) * group * rows, group * rows, 0)

    def to_head_group(values):
        depth = values.shape[1] // group
        blocks = jnp.transpose(values.reshape(values.shape[0], group, depth), (1, 0, 2))
        blocks = jnp.broadcast_to(blocks[None], (groups,) + blocks.shape)
        return exchange(blocks.reshape((n,) + blocks.shape[2:])).reshape(-1, depth)

    def from_head_group(values):
        depth = values.shape[1]
        got = exchange(values.astype(BF16).reshape(n, -1, depth)).astype(F32)
        got = jnp.sum(got.reshape(groups, group, -1, depth), axis=0)
        return jnp.transpose(got, (1, 0, 2)).reshape(-1, group * depth)

    gains = exchange(
        jnp.broadcast_to(
            jnp.concatenate([norm1_gain, norm2_gain, q_gain, kv_gain])[None],
            (n, 2 * own_d + q_gain.shape[0] + kv_gain.shape[0]),
        )
    )
    pad = -(latents + experts) % 128
    down_own = jnp.concatenate(
        [query_down_weight, kv_down, router, jnp.zeros((own_d, pad), BF16)], axis=1
    )
    if rows == own_d:
        gathered = (gather_rows(jnp.concatenate([layer_input, down_own], axis=1)),)
    else:
        gathered = (gather_rows(layer_input), gather_rows(down_own))
    ff_own = shared_gate.shape[1] // n
    shared_stack = jnp.stack([shared_gate, shared_up, shared_down], axis=0)
    shared_blocks = jnp.transpose(shared_stack.reshape(3, own_d, n, ff_own), (2, 0, 1, 3))
    gathered, kv_up_heads, q_up_heads, gains, late = lax.optimization_barrier(
        (
            gathered,
            to_head_group(kv_up),
            to_head_group(q_up),
            gains,
            (half_rows(grad_output), out_proj, shared_blocks),
        )
    )
    go_half, out_late, shared_late = late
    go_all = lax.all_gather(go_half, ("ctx", "wt"), axis=0, tiled=True)
    out_heads = to_head_group(out_late)
    shared_got = exchange(shared_late)
    if rows == own_d:
        x_all, down_all = gathered[0][:, :width], gathered[0][:, width:]
    else:
        x_all, down_all = gathered
    q_down_all = down_all[:, :qr]
    kv_down_all = down_all[:, qr:latents]
    router_all = down_all[:, latents : latents + experts]
    norm1_full = gains[:, :own_d].reshape(-1).astype(F32)
    norm2_full = gains[:, own_d : 2 * own_d].reshape(-1).astype(F32)
    qgain_full = gains[:, 2 * own_d : 2 * own_d + own_q].reshape(-1).astype(F32)
    kvgain_full = gains[:, 2 * own_d + own_q :].reshape(-1).astype(F32)

    key_positions = positions_of(block_table)
    query_positions = own_group(key_positions)
    own_positions = positions_of(lax.dynamic_slice_in_dim(block_table, c, 1, 0))
    cosine_all, sine_all = rope_tables(key_positions)
    cosine_group, sine_group = rope_tables(query_positions)
    cosine, sine = rope_tables(own_positions)

    normed_all = normalize(x_all.astype(F32), norm1_full)[0].astype(BF16)
    kv_latent_all = dot(normed_all, kv_down_all)
    latent_all = normalize(kv_latent_all[:, :kvr], kvgain_full)[0].astype(BF16)
    rope_all = rotate(kv_latent_all[:, kvr:], cosine_all, sine_all).astype(BF16)
    q_normed_group = normalize(dot(own_group(normed_all), q_down_all), qgain_full)[0].astype(BF16)
    query_f = dot(q_normed_group, q_up_heads)
    key_values = dot(latent_all, kv_up_heads).astype(BF16)
    allowed = query_positions[:, None] >= key_positions[None, :]
    queries, keys, values_heads, exacts, attended = [], [], [], [], []
    for h in range(own_heads):
        query_h = query_f[:, h * head_dim : (h + 1) * head_dim]
        query_h = jnp.concatenate(
            [query_h[:, :NOPE], rotate(query_h[:, NOPE:], cosine_group, sine_group)], axis=-1
        ).astype(BF16)
        kv_h = key_values[:, h * (NOPE + VDIM) : (h + 1) * (NOPE + VDIM)]
        keys_h = jnp.concatenate([kv_h[:, :NOPE], rope_all], axis=-1)
        scores = dot_rows(query_h, keys_h) * score_scale
        log_total = jnp.log(
            jnp.sum(jnp.where(allowed, jnp.exp(scores), 0.0), axis=-1, keepdims=True)
        )
        exact = jnp.where(allowed, jnp.exp(scores - log_total), 0.0)
        queries.append(query_h)
        keys.append(keys_h)
        values_heads.append(kv_h[:, NOPE:])
        exacts.append(exact)
        attended.append(dot(exact.astype(BF16), kv_h[:, NOPE:]).astype(BF16))
    attention = jnp.concatenate(attended, axis=1)

    inputs = layer_input.astype(F32)
    hidden_one = inputs + group_sum(dot_rows(attention, out_heads))
    normed2_f, inverse_two = normalize(hidden_one, norm2_full)
    normed_two = normed2_f.astype(BF16)
    sigma = jax.nn.sigmoid(dot(normed_two, router_all))
    expert_ids = jnp.arange(experts, dtype=jnp.int32)
    picked = jnp.any(routes[..., None] == expert_ids[None, None, :], axis=1)
    chosen = jnp.where(picked, sigma, 0.0)
    chosen_total = jnp.sum(chosen, axis=-1, keepdims=True)
    gates = route_scale * chosen / chosen_total
    gates_high = gates.astype(BF16)
    gates_low = (gates - gates_high.astype(F32)).astype(BF16)
    gates_pad = jnp.zeros((rows, -2 * experts % 128), BF16)
    sent_rows = jnp.concatenate([normed_two, gates_high, gates_low, gates_pad], axis=1)
    sent_rows, go_all, shared_got = lax.optimization_barrier((sent_rows, go_all, shared_got))
    shared_own = jnp.transpose(shared_got, (1, 0, 2, 3)).reshape(3, width, ff_own)
    got_rows = gather_rows(sent_rows)
    normed_two_all = got_rows[:, :width]
    got_gates = got_rows[:, width : width + 2 * experts].astype(F32)
    is_own = (jnp.arange(2 * experts) % experts == c)[None]
    gate_own = jnp.sum(jnp.where(is_own, got_gates, 0.0), axis=-1, keepdims=True)

    e_gate, e_up, e_down = expert_gate[0], routed_expert_up_weight[0], expert_down[0]
    ff = e_gate.shape[1]
    s_gate, s_up, s_down = shared_own[0], shared_own[1], jnp.transpose(shared_own[2])
    gate_mat = jnp.concatenate([e_gate, s_gate], axis=1)
    up_mat = jnp.concatenate([e_up, s_up], axis=1)
    down_mat = jnp.concatenate([e_down, s_down], axis=0)
    back_unit = dot_rows(go_all, down_mat)
    gate_pre = dot(normed_two_all, gate_mat)
    up_pre = dot(normed_two_all, up_mat)
    act, slope = silu_parts(gate_pre)
    hidden = act * up_pre
    is_expert = (jnp.arange(ff + ff_own) < ff)[None]
    scale = jnp.where(is_expert, gate_own, 1.0)
    hidden_scaled = (hidden * scale).astype(BF16)
    back = back_unit * scale
    d_gate = (back * up_pre * slope).astype(BF16)
    d_up = (back * act).astype(BF16)
    grad_gate_own = jnp.sum(jnp.where(is_expert, back_unit * hidden, 0.0), axis=-1)
    d_normed = dot_rows(
        jnp.concatenate([d_gate, d_up], axis=1), jnp.concatenate([gate_mat, up_mat], axis=1)
    )
    d_normed, grad_gate_own, d_gate, d_up, hidden_scaled = lax.optimization_barrier(
        (d_normed.astype(BF16), grad_gate_own, d_gate, d_up, hidden_scaled)
    )
    grad_normed_two, results = ring_sum(
        d_normed,
        n,
        w,
        place,
        (
            lambda: dot(hidden_scaled, down_mat).astype(BF16),
            lambda: (
                dot_cols(normed_two_all, d_gate),
                exchange(wt_sum(grad_gate_own).reshape(n, rows)),
            ),
            lambda: dot_cols(normed_two_all, d_up),
            lambda: dot_cols(hidden_scaled, go_all),
        ),
    )
    ffn_part, (d_gate_mat, grad_gates), d_up_mat, d_down_mat = results
    grad_normed_two = both_halves(grad_normed_two.astype(BF16), 0).astype(F32)
    grad_expert_gate = d_gate_mat[None, :, :ff]
    grad_expert_up = d_up_mat[None, :, :ff]
    grad_expert_down = d_down_mat[None, :ff]
    d_shared = jnp.stack(
        [d_gate_mat[:, ff:], d_up_mat[:, ff:], jnp.transpose(d_down_mat[ff:])], axis=0
    )
    d_shared = jnp.transpose(d_shared.reshape(3, n, own_d, ff_own), (1, 0, 2, 3)).astype(BF16)
    d_shared = jnp.transpose(exchange(d_shared), (1, 2, 0, 3)).reshape(3, own_d, n * ff_own)

    grad_gates = jnp.where(picked, jnp.transpose(grad_gates), 0.0)
    grad_chosen = (
        route_scale * grad_gates - jnp.sum(grad_gates * gates, axis=-1, keepdims=True)
    ) / chosen_total
    grad_logits = (grad_chosen * chosen * (1.0 - chosen)).astype(BF16)
    upstream = grad_output.astype(F32)
    grad_normed_two = grad_normed_two + dot_rows(grad_logits, router_all)
    grad_router_part = dot_cols(grad_logits, normed_two)
    grad_hidden, norm2_part = norm_backward(grad_normed_two, hidden_one, inverse_two, norm2_full)
    grad_hidden = grad_hidden + upstream
    grad_hidden_half = grad_hidden.astype(BF16)
    hidden_group = group_gather(grad_hidden_half)
    hidden_group, ffn_part = lax.optimization_barrier((hidden_group, ffn_part))
    cols = width // wt
    ffn_theirs = other_wt(lax.dynamic_slice_in_dim(ffn_part, (1 - w) * cols, cols, 1))
    ffn_mine = lax.dynamic_slice_in_dim(ffn_part, w * cols, cols, 1)
    ffn_out = lax.psum_scatter(ffn_mine + ffn_theirs, "ctx", scatter_dimension=0, tiled=True)
    grad_attention = dot(hidden_group, out_heads).astype(BF16)

    query_parts, kv_parts, rope_part = [], [], 0.0
    for h in range(own_heads):
        grad_att = grad_attention[:, h * VDIM : (h + 1) * VDIM]
        delta = jnp.sum(grad_att.astype(F32) * attended[h].astype(F32), axis=-1, keepdims=True)
        grad_probs = dot_rows(grad_att, values_heads[h])
        grad_scores = (exacts[h] * (grad_probs - delta)).astype(BF16)
        grad_query = score_scale * dot(grad_scores, keys[h])
        grad_keys = score_scale * dot_cols(grad_scores, queries[h])
        grad_values = dot_cols(exacts[h].astype(BF16), grad_att)
        query_parts.append(grad_query[:, :NOPE])
        query_parts.append(unrotate(grad_query[:, NOPE:], cosine_group, sine_group))
        kv_parts.append(grad_keys[:, :NOPE])
        kv_parts.append(grad_values)
        rope_part = rope_part + grad_keys[:, NOPE:]
    grad_query_half = jnp.concatenate(query_parts, axis=-1).astype(BF16)
    grad_kv_heads = jnp.concatenate(kv_parts, axis=-1).astype(BF16)
    kv_part = jnp.concatenate([dot_rows(grad_kv_heads, kv_up_heads), rope_part], axis=1)
    kv_part = kv_part.astype(BF16).reshape(n, wt, rows // wt, kvr + ROPE)
    kv_theirs = other_wt(lax.dynamic_index_in_dim(kv_part, 1 - w, 1, keepdims=False))
    kv_part = lax.dynamic_index_in_dim(kv_part, w, 1, keepdims=False) + kv_theirs
    kv_part, d_shared = lax.optimization_barrier((kv_part, d_shared))
    kv_own = both_halves(jnp.sum(exchange(kv_part).astype(F32), axis=0), 0)
    grad_q_normed = group_sum(dot_rows(grad_query_half, q_up_heads))
    d_shared = d_shared.astype(F32)

    normed_f, inverse_one = normalize(inputs, norm1_full)
    normed = normed_f.astype(BF16)
    q_latent = dot(normed, q_down_all)
    q_inverse = normalize(q_latent, qgain_full)[1]
    kv_latent = dot(normed, kv_down_all)[:, :kvr]
    kv_inverse = normalize(kv_latent, kvgain_full)[1]
    grad_q_latent, qgain_part = norm_backward(grad_q_normed, q_latent, q_inverse, qgain_full)
    grad_kv_part, kvgain_part = norm_backward(
        kv_own[:, :kvr], kv_latent, kv_inverse, kvgain_full
    )
    grad_rope_raw = unrotate(kv_own[:, kvr:], cosine, sine)
    grad_latents = jnp.concatenate([grad_q_latent, grad_kv_part, grad_rope_raw], axis=-1).astype(
        BF16
    )
    own_cols = -(-latents // (n * wt))
    col_blocks = jnp.pad(grad_latents, ((0, 0), (0, own_cols * n * wt - latents)))
    col_blocks = jnp.transpose(col_blocks.reshape(rows, n, wt, own_cols), (2, 1, 0, 3))
    col_blocks = lax.dynamic_index_in_dim(col_blocks, w, 0, keepdims=False)
    latent_cols = exchange(col_blocks).reshape(tokens, own_cols)
    ffn_out = lax.optimization_barrier((ffn_out, grad_latents))[0]
    output = (hidden_one + both_halves(ffn_out, 1).astype(F32)).astype(BF16)
    grad_normed = dot_rows(grad_latents, down_all[:, :latents])
    grad_input, norm1_part = norm_backward(grad_normed, inputs, inverse_one, norm1_full)
    grad_input = grad_input + grad_hidden
    down_cols = dot_cols(latent_cols, normed_all).reshape(own_cols, n, own_d)
    down_cols = jnp.transpose(down_cols, (1, 0, 2))

    grad_out_proj = from_head_group(dot_cols(hidden_group, attention))
    grad_q_up = from_head_group(dot_cols(q_normed_group, grad_query_half))
    grad_kv_up = from_head_group(dot_cols(latent_all, grad_kv_heads))
    small = jnp.concatenate(
        [
            norm1_part.reshape(n, -1),
            norm2_part.reshape(n, -1),
            qgain_part.reshape(n, -1),
            kvgain_part.reshape(n, -1),
            jnp.transpose(grad_router_part.reshape(experts, n, own_d), (1, 0, 2)).reshape(n, -1),
        ],
        axis=1,
    )
    last = exchange(jnp.concatenate([down_cols, small.reshape(n, -1, own_d)], axis=1))
    small = jnp.sum(last[:, own_cols:], axis=0).reshape(-1)
    down_mine = last[:, :own_cols]
    down_theirs = other_wt(down_mine)
    grad_down = jnp.stack(
        [jnp.where(w == 0, down_mine, down_theirs), jnp.where(w == 0, down_theirs, down_mine)],
        axis=1,
    )
    grad_down = jnp.transpose(grad_down.reshape(-1, own_d)[:latents])
    edge = 2 * own_d + own_q
    edge_kv = edge + kv_gain.shape[0]
    return (
        output,
        grad_input,
        small[:own_d],
        grad_down[:, :qr],
        small[2 * own_d : edge],
        grad_q_up,
        grad_down[:, qr:],
        small[edge:edge_kv],
        grad_kv_up,
        grad_out_proj,
        small[own_d : 2 * own_d],
        jnp.transpose(small[edge_kv:].reshape(experts, own_d)),
        d_shared[0],
        d_shared[1],
        d_shared[2],
        grad_expert_gate,
        grad_expert_up,
        grad_expert_down,
    )


def solution(mesh):
    placed = (
        P("ctx", None),
        P(),
        P("ctx", None),
        P("ctx", None),
        P("ctx"),
        P("ctx", None),
        P("ctx"),
        P("ctx", "wt"),
        P("ctx", None),
        P("ctx"),
        P("ctx", "wt"),
        P("ctx", "wt"),
        P("ctx"),
        P("ctx", None),
        P("ctx", "wt"),
        P("ctx", "wt"),
        P("ctx", "wt"),
        P("ctx", None, "wt"),
        P("ctx", None, "wt"),
        P("ctx", "wt", None),
    )
    return jax.shard_map(
        body,
        mesh=mesh,
        in_specs=placed,
        out_specs=(
            P("ctx", None),
            P("ctx", None),
            P("ctx"),
            P("ctx", None),
            P("ctx"),
            P("ctx", "wt"),
            P("ctx", None),
            P("ctx"),
            P("ctx", "wt"),
            P("ctx", "wt"),
            P("ctx"),
            P("ctx", None),
            P("ctx", "wt"),
            P("ctx", "wt"),
            P("ctx", "wt"),
            P("ctx", None, "wt"),
            P("ctx", None, "wt"),
            P("ctx", "wt", None),
        ),
        check_vma=False,
    )
```

```python
import math

import jax
import jax.numpy as jnp
from jax import lax
from jax.sharding import PartitionSpec as P


NOPE = 128
ROPE = 64
VDIM = 128
BLOCK = 64

rms_epsilon = 1e-06
rope_base = 50000.0
route_scale = 2.446


F32 = jnp.float32
BF16 = jnp.bfloat16


def dot(left_mat, right_mat):
    return lax.dot_general(
        left_mat, right_mat, (((1,), (0,)), ((), ())), preferred_element_type=F32
    )


def dot_rows(left_mat, right_mat):
    return lax.dot_general(
        left_mat, right_mat, (((1,), (1,)), ((), ())), preferred_element_type=F32
    )


def dot_cols(left_mat, right_mat):
    return lax.dot_general(
        left_mat, right_mat, (((0,), (0,)), ((), ())), preferred_element_type=F32
    )


def normalize(values, weights):
    inverse = lax.rsqrt(jnp.mean(values * values, axis=-1, keepdims=True) + rms_epsilon)
    return (values * inverse * weights, inverse)


def norm_backward(upstream, values, inverse, weights):
    unit_rows = values * inverse
    scaled = upstream * weights
    inner_mean = jnp.mean(scaled * unit_rows, axis=-1, keepdims=True)
    return (inverse * (scaled - unit_rows * inner_mean), jnp.sum(upstream * unit_rows, axis=0))


def rope_tables(positions):
    half_dim = ROPE // 2
    exponent = jnp.arange(half_dim, dtype=F32) * (2.0 / ROPE)
    frequency = jnp.exp(-exponent * math.log(rope_base))
    angles = positions.astype(F32)[:, None] * frequency[None, :]
    return (jnp.cos(angles), jnp.sin(angles))


def rotate(values, cosine, sine_part):
    half_dim = values.shape[-1] // 2
    first_half = values[..., :half_dim]
    second_half = values[..., half_dim:]
    return jnp.concatenate(
        [
            first_half * cosine - second_half * sine_part,
            first_half * sine_part + second_half * cosine,
        ],
        axis=-1,
    )


def unrotate(values, cosine, sine_part):
    return rotate(values, cosine, -sine_part)


def silu_parts(values):
    sigma = jax.nn.sigmoid(values)
    return (values * sigma, sigma * (1.0 + values * (1.0 - sigma)))


def positions_of(table_rows):
    offsets = jnp.arange(BLOCK, dtype=jnp.int32)
    return (table_rows[:, :, None] * BLOCK + offsets[None, None, :]).reshape(-1)


CTX = ("line", "plane")


def exchange(blocks, axes=CTX):
    return lax.all_to_all(blocks, axes, split_axis=0, concat_axis=0, tiled=True)


def wt_sum(values):
    return values + other_wt(values)


def other_wt(values):
    return lax.ppermute(values, "wt", [(0, 1), (1, 0)])


def layer(
    layer_input,
    block_table,
    routes,
    grad_output,
    norm1_gain,
    query_down_weight,
    q_gain,
    q_up,
    kv_down,
    kv_gain,
    kv_up,
    out_proj,
    norm2_gain,
    router,
    shared_gate,
    shared_up,
    shared_down,
    expert_gate,
    routed_expert_up_weight,
    expert_down,
):
    n = lax.axis_size(CTX)
    wt = lax.axis_size("wt")
    c = lax.axis_index(CTX)
    w = lax.axis_index("wt")
    rows, width = layer_input.shape
    tokens = n * rows
    kvr = kv_gain.shape[0] * n
    qr = q_gain.shape[0] * n
    head_dim = NOPE + ROPE
    heads = q_up.shape[1] // head_dim
    group = lax.axis_size("plane")
    groups = lax.axis_size("line")
    own_heads = heads // group
    g = lax.axis_index("plane")
    experts = router.shape[1]
    own_d = norm1_gain.shape[0]
    own_q = q_gain.shape[0]
    latents = qr + kvr + ROPE
    score_scale = head_dim ** (-0.5)

    def half_rows(values):
        size = values.shape[0] // wt
        return lax.dynamic_slice_in_dim(values, w * size, size, 0)

    def gather_rows(values):
        return lax.all_gather(half_rows(values), CTX + ("wt",), axis=0, tiled=True)

    def gather_tokens(mine):
        return lax.all_gather(mine, ("plane", "wt", "line"), axis=0, tiled=True)

    def scatter_tokens(values, beside=()):
        some = lax.psum_scatter(values, ("plane", "wt"), scatter_dimension=0, tiled=True)
        some, beside = lax.optimization_barrier((some, beside))
        return lax.psum_scatter(some, "line", scatter_dimension=0, tiled=True), beside

    def both_halves(mine, axis):
        theirs = other_wt(mine)
        first, second = jnp.where(w == 0, mine, theirs), jnp.where(w == 0, theirs, mine)
        return jnp.concatenate([first, second], axis=axis)

    def group_moves(k):
        return [(i, i ^ k) for i in range(group)]

    def group_sum(values):
        cols = values.shape[1] // 2
        sent = lax.dynamic_slice_in_dim(values, (1 - w) * cols, cols, 1).astype(BF16)
        total = lax.dynamic_slice_in_dim(values, w * cols, cols, 1)
        total = (total + other_wt(sent).astype(F32)).reshape(group, rows, cols)
        own = lax.dynamic_index_in_dim(total, g, 0, keepdims=False)
        for k in range(1, group):
            block = lax.dynamic_index_in_dim(total, g ^ k, 0, keepdims=False).astype(BF16)
            own = own + lax.ppermute(block, "plane", group_moves(k)).astype(F32)
        return both_halves(own, 1)

    def group_gather(values):
        cols = values.shape[1] // 2
        mine = lax.dynamic_slice_in_dim(values, w * cols, cols, 1)
        out = jnp.zeros((group, rows, cols), values.dtype)
        out = lax.dynamic_update_index_in_dim(out, mine, g, 0)
        for k in range(1, group):
            got = lax.ppermute(mine, "plane", group_moves(k))
            out = lax.dynamic_update_index_in_dim(out, got, g ^ k, 0)
        return both_halves(out.reshape(group * rows, cols), 1)

    def own_group(values):
        start = lax.axis_index("line") * group * rows
        return lax.dynamic_slice_in_dim(values, start, group * rows, 0)

    lanes = 128

    def to_head_group(values):
        depth = values.shape[1] // group
        blocks = jnp.transpose(values.reshape(values.shape[0], group, depth), (1, 0, 2))
        blocks = jnp.broadcast_to(blocks[None], (groups,) + blocks.shape)
        return exchange(blocks.reshape((n,) + blocks.shape[2:])).reshape(-1, depth)

    def from_head_groups(terms):
        packed, shapes = [], []
        for values in terms:
            k, depth = values.shape[0] // n, values.shape[1]
            split = values.astype(BF16).reshape(groups, group, k, depth // lanes, lanes)
            split = jnp.transpose(split, (0, 1, 3, 2, 4))
            packed.append(split.reshape(groups, group, -1, lanes))
            shapes.append((k, depth // lanes))
        packed = jnp.concatenate(packed, axis=2)
        summed = lax.psum_scatter(
            packed.reshape(-1, lanes), "line", scatter_dimension=0, tiled=True
        )
        got = exchange(summed.reshape(group, -1, lanes), "plane")

        def finish(got):
            out, at = [], 0
            for k, blocks in shapes:
                part = got[:, at : at + k * blocks].reshape(group, blocks, k, lanes)
                out.append(jnp.transpose(part, (2, 0, 1, 3)).reshape(k, -1).astype(F32))
                at += k * blocks
            return out

        return got, finish

    gains = exchange(
        jnp.broadcast_to(
            jnp.concatenate([norm1_gain, norm2_gain, q_gain, kv_gain])[None],
            (n, 2 * own_d + q_gain.shape[0] + kv_gain.shape[0]),
        )
    )
    pad = -(latents + experts) % 128
    down_own = jnp.concatenate(
        [query_down_weight, kv_down, router, jnp.zeros((own_d, pad), BF16)], axis=1
    )
    if rows == own_d:
        gathered = (gather_rows(jnp.concatenate([layer_input, down_own], axis=1)),)
    else:
        gathered = (gather_rows(layer_input), gather_rows(down_own))
    ff_own = shared_gate.shape[1] // n
    shared_stack = jnp.stack([shared_gate, shared_up, shared_down], axis=0)
    shared_blocks = jnp.transpose(shared_stack.reshape(3, own_d, n, ff_own), (2, 0, 3, 1))
    gathered, kv_up_heads, q_up_heads, out_heads, gains, late = lax.optimization_barrier(
        (
            gathered,
            to_head_group(kv_up),
            to_head_group(q_up),
            to_head_group(out_proj),
            gains,
            (half_rows(grad_output), shared_blocks),
        )
    )
    go_half, shared_late = late
    go_all = gather_tokens(go_half)
    shared_got = exchange(shared_late)
    if rows == own_d:
        x_all, down_all = gathered[0][:, :width], gathered[0][:, width:]
    else:
        x_all, down_all = gathered
    q_down_all = down_all[:, :qr]
    kv_down_all = down_all[:, qr:latents]
    router_all = down_all[:, latents : latents + experts]
    norm1_full = gains[:, :own_d].reshape(-1).astype(F32)
    norm2_full = gains[:, own_d : 2 * own_d].reshape(-1).astype(F32)
    qgain_full = gains[:, 2 * own_d : 2 * own_d + own_q].reshape(-1).astype(F32)
    kvgain_full = gains[:, 2 * own_d + own_q :].reshape(-1).astype(F32)

    key_positions = positions_of(block_table)
    query_positions = own_group(key_positions)
    own_positions = positions_of(lax.dynamic_slice_in_dim(block_table, c, 1, 0))
    cosine_all, sine_all = rope_tables(key_positions)
    cosine_group, sine_group = rope_tables(query_positions)
    cosine, sine = rope_tables(own_positions)

    normed_all = lax.optimization_barrier(
        normalize(x_all.astype(F32), norm1_full)[0].astype(BF16)
    )
    kv_latent_all = dot(normed_all, kv_down_all)
    latent_all = normalize(kv_latent_all[:, :kvr], kvgain_full)[0].astype(BF16)
    rope_all = rotate(kv_latent_all[:, kvr:], cosine_all, sine_all).astype(BF16)
    q_normed_group = normalize(dot(own_group(normed_all), q_down_all), qgain_full)[0].astype(BF16)
    query_f = dot(q_normed_group, q_up_heads)
    key_values = dot(latent_all, kv_up_heads).astype(BF16)
    allowed = query_positions[:, None] >= key_positions[None, :]
    queries, keys, values_heads, exacts, attended = [], [], [], [], []
    for h in range(own_heads):
        query_h = query_f[:, h * head_dim : (h + 1) * head_dim]
        query_h = jnp.concatenate(
            [query_h[:, :NOPE], rotate(query_h[:, NOPE:], cosine_group, sine_group)], axis=-1
        ).astype(BF16)
        kv_h = key_values[:, h * (NOPE + VDIM) : (h + 1) * (NOPE + VDIM)]
        keys_h = jnp.concatenate([kv_h[:, :NOPE], rope_all], axis=-1)
        scores = dot_rows(query_h, keys_h) * score_scale
        log_total = jnp.log(
            jnp.sum(jnp.where(allowed, jnp.exp(scores), 0.0), axis=-1, keepdims=True)
        )
        exact = jnp.where(allowed, jnp.exp(scores - log_total), 0.0)
        queries.append(query_h)
        keys.append(keys_h)
        values_heads.append(kv_h[:, NOPE:])
        exacts.append(exact)
        attended.append(dot(exact.astype(BF16), kv_h[:, NOPE:]).astype(BF16))
    attention = jnp.concatenate(attended, axis=1)
    attention, shared_got = lax.optimization_barrier((attention, shared_got))

    inputs = layer_input.astype(F32)
    hidden_one = inputs + group_sum(dot_rows(attention, out_heads))
    normed2_f, inverse_two = normalize(hidden_one, norm2_full)
    normed_two = normed2_f.astype(BF16)
    sigma = jax.nn.sigmoid(dot(normed_two, router_all))
    expert_ids = jnp.arange(experts, dtype=jnp.int32)
    picked = jnp.any(routes[..., None] == expert_ids[None, None, :], axis=1)
    chosen = jnp.where(picked, sigma, 0.0)
    chosen_total = jnp.sum(chosen, axis=-1, keepdims=True)
    gates = route_scale * chosen / chosen_total
    gates_high = gates.astype(BF16)
    gates_low = (gates - gates_high.astype(F32)).astype(BF16)
    gates_pad = jnp.zeros((rows, -2 * experts % 128), BF16)
    sent_rows = jnp.concatenate([normed_two, gates_high, gates_low, gates_pad], axis=1)
    sent_rows, go_all = lax.optimization_barrier((sent_rows, go_all))
    got_rows = gather_tokens(half_rows(sent_rows))

    e_gate, e_up = jnp.transpose(expert_gate[0]), jnp.transpose(routed_expert_up_weight[0])
    ff = e_gate.shape[0]
    ff_all = ff + ff_own
    s_gate, s_up, s_down = jnp.transpose(shared_got, (1, 2, 0, 3)).reshape(3, ff_own, width)
    mats = jnp.concatenate([e_gate, s_gate, e_up, s_up, expert_down[0], s_down], axis=0)
    back_unit = dot_rows(go_all, mats[2 * ff_all :])
    normed_f, inverse_one = normalize(inputs, norm1_full)
    normed = normed_f.astype(BF16)
    q_latent = dot(normed, q_down_all)
    q_inverse = normalize(q_latent, qgain_full)[1]
    kv_latent = dot(normed, kv_down_all)[:, :kvr]
    kv_inverse = normalize(kv_latent, kvgain_full)[1]
    normed_half = lax.dynamic_index_in_dim(
        normed_all.reshape(n, wt, rows // wt, width), w, 1, keepdims=False
    ).reshape(tokens // wt, width)
    ready = (mats, back_unit, inverse_one, q_latent, q_inverse, kv_latent, kv_inverse, normed_half)
    got_rows, ready = lax.optimization_barrier((got_rows, ready))
    mats, back_unit, inverse_one, q_latent, q_inverse, kv_latent, kv_inverse, normed_half = ready
    normed_two_all = got_rows[:, :width]
    got_gates = got_rows[:, width : width + 2 * experts].astype(F32)
    is_own = (jnp.arange(2 * experts) % experts == c)[None]
    gate_own = jnp.sum(jnp.where(is_own, got_gates, 0.0), axis=-1, keepdims=True)

    gate_pre = dot_rows(normed_two_all, mats[:ff_all])
    up_pre = dot_rows(normed_two_all, mats[ff_all : 2 * ff_all])
    act, slope = silu_parts(gate_pre)
    hidden = act * up_pre
    is_expert = (jnp.arange(ff_all) < ff)[None]
    scale = jnp.where(is_expert, gate_own, 1.0)
    hidden_scaled = (hidden * scale).astype(BF16)
    back = back_unit * scale
    d_gate = (back * up_pre * slope).astype(BF16)
    d_up = (back * act).astype(BF16)
    grad_gate_own = jnp.sum(jnp.where(is_expert, back_unit * hidden, 0.0), axis=-1)
    d_normed = dot(jnp.concatenate([d_gate, d_up], axis=1), mats[: 2 * ff_all])
    d_normed, grad_gate_own, d_gate, d_up, hidden_scaled = lax.optimization_barrier(
        (d_normed.astype(BF16), grad_gate_own, d_gate, d_up, hidden_scaled)
    )
    ffn_part = dot(hidden_scaled, mats[2 * ff_all :]).astype(BF16)
    grad_expert_gate = dot_cols(d_gate[:, :ff], normed_two_all)
    grad_expert_up = dot_cols(d_up[:, :ff], normed_two_all)
    grad_expert_down = dot_cols(hidden_scaled[:, :ff], go_all)
    grad_gates = wt_sum(grad_gate_own).reshape(group, wt, groups, rows // wt)
    grad_gates = exchange(jnp.transpose(grad_gates, (2, 0, 1, 3)).reshape(n, rows))
    grad_expert_gate = jnp.transpose(grad_expert_gate)[None]
    grad_expert_up = jnp.transpose(grad_expert_up)[None]
    grad_expert_down = grad_expert_down[None]
    d_shared_in = dot_cols(jnp.concatenate([d_gate[:, ff:], d_up[:, ff:]], axis=1), normed_two_all)
    d_shared_out = dot_cols(hidden_scaled[:, ff:], go_all)
    d_shared = jnp.concatenate([d_shared_in, d_shared_out], axis=0).astype(BF16)
    d_shared = jnp.transpose(d_shared.reshape(3, ff_own, n, own_d), (2, 0, 1, 3))
    d_shared = exchange(d_shared)
    grad_normed_half, (d_shared, grad_gates, ffn_part, grad_expert_gate) = scatter_tokens(
        d_normed, (d_shared, grad_gates, ffn_part, grad_expert_gate)
    )
    grad_normed_half, ffn_part, grad_expert_up, grad_expert_down = lax.optimization_barrier(
        (grad_normed_half, ffn_part, grad_expert_up, grad_expert_down)
    )
    ffn_half = scatter_tokens(ffn_part)[0]
    grad_normed_two = both_halves(grad_normed_half, 0).astype(F32)

    grad_gates = jnp.where(picked, jnp.transpose(grad_gates), 0.0)
    grad_chosen = (
        route_scale * grad_gates - jnp.sum(grad_gates * gates, axis=-1, keepdims=True)
    ) / chosen_total
    grad_logits = (grad_chosen * chosen * (1.0 - chosen)).astype(BF16)
    upstream = grad_output.astype(F32)
    grad_normed_two = grad_normed_two + dot_rows(grad_logits, router_all)
    grad_router_part = dot_cols(grad_logits, normed_two)
    grad_hidden, norm2_part = norm_backward(grad_normed_two, hidden_one, inverse_two, norm2_full)
    grad_hidden = grad_hidden + upstream
    grad_hidden_half = grad_hidden.astype(BF16)
    hidden_group = group_gather(grad_hidden_half)
    grad_attention = dot(hidden_group, out_heads).astype(BF16)

    query_parts, kv_parts, rope_part = [], [], 0.0
    for h in range(own_heads):
        grad_att = grad_attention[:, h * VDIM : (h + 1) * VDIM]
        delta = jnp.sum(grad_att.astype(F32) * attended[h].astype(F32), axis=-1, keepdims=True)
        grad_probs = dot_rows(grad_att, values_heads[h])
        grad_scores = (exacts[h] * (grad_probs - delta)).astype(BF16)
        grad_query = score_scale * dot(grad_scores, keys[h])
        grad_keys = score_scale * dot_cols(grad_scores, queries[h])
        grad_values = dot_cols(exacts[h].astype(BF16), grad_att)
        query_parts.append(grad_query[:, :NOPE])
        query_parts.append(unrotate(grad_query[:, NOPE:], cosine_group, sine_group))
        kv_parts.append(grad_keys[:, :NOPE])
        kv_parts.append(grad_values)
        rope_part = rope_part + grad_keys[:, NOPE:]
    grad_query_half = jnp.concatenate(query_parts, axis=-1).astype(BF16)
    grad_kv_heads = jnp.concatenate(kv_parts, axis=-1).astype(BF16)
    kv_part = jnp.concatenate([dot_rows(grad_kv_heads, kv_up_heads), rope_part], axis=1)
    kv_part = kv_part.astype(BF16).reshape(n, wt, rows // wt, kvr + ROPE)
    kv_theirs = other_wt(lax.dynamic_index_in_dim(kv_part, 1 - w, 1, keepdims=False))
    kv_part = lax.dynamic_index_in_dim(kv_part, w, 1, keepdims=False) + kv_theirs
    kv_got, grad_q_normed = lax.optimization_barrier(
        (exchange(kv_part), group_sum(dot_rows(grad_query_half, q_up_heads)))
    )
    kv_own = both_halves(jnp.sum(kv_got.astype(F32), axis=0), 0)
    weight_terms, kv_own = lax.optimization_barrier(
        (
            (
                dot_cols(hidden_group, attention).astype(BF16),
                dot_cols(q_normed_group, grad_query_half).astype(BF16),
                dot_cols(latent_all, grad_kv_heads).astype(BF16),
            ),
            kv_own,
        )
    )
    heads_back, heads_finish = from_head_groups(weight_terms)
    d_shared = jnp.transpose(d_shared, (1, 3, 0, 2)).reshape(3, own_d, n * ff_own).astype(F32)

    grad_q_latent, qgain_part = norm_backward(grad_q_normed, q_latent, q_inverse, qgain_full)
    grad_kv_part, kvgain_part = norm_backward(
        kv_own[:, :kvr], kv_latent, kv_inverse, kvgain_full
    )
    grad_rope_raw = unrotate(kv_own[:, kvr:], cosine, sine)
    grad_latents = jnp.concatenate([grad_q_latent, grad_kv_part, grad_rope_raw], axis=-1).astype(
        BF16
    )
    own_cols = -(-latents // (8 * n * wt)) * 8
    col_blocks = jnp.pad(half_rows(grad_latents), ((0, 0), (0, own_cols * n * wt - latents)))
    col_blocks = jnp.transpose(col_blocks.reshape(rows // wt, n, wt * own_cols), (1, 0, 2))
    latent_cols = exchange(col_blocks).reshape(tokens // wt, wt * own_cols)
    grad_normed = dot_rows(grad_latents, down_all[:, :latents])
    grad_input, norm1_part = norm_backward(grad_normed, inputs, inverse_one, norm1_full)
    grad_input = grad_input + grad_hidden
    down_cols = dot_cols(latent_cols, normed_half)
    down_theirs = other_wt(lax.dynamic_slice_in_dim(down_cols, (1 - w) * own_cols, own_cols, 0))
    down_cols = lax.dynamic_slice_in_dim(down_cols, w * own_cols, own_cols, 0) + down_theirs
    down_cols = jnp.transpose(down_cols.reshape(own_cols, n, own_d), (1, 0, 2))

    small = jnp.concatenate(
        [
            norm1_part.reshape(n, -1),
            norm2_part.reshape(n, -1),
            qgain_part.reshape(n, -1),
            kvgain_part.reshape(n, -1),
            jnp.transpose(grad_router_part.reshape(experts, n, own_d), (1, 0, 2)).reshape(n, -1),
        ],
        axis=1,
    )
    last = jnp.concatenate([down_cols, small.reshape(n, -1, own_d)], axis=1)
    last = exchange(last.astype(BF16))
    last, heads_back = lax.optimization_barrier((last, heads_back))
    grad_out_proj, grad_q_up, grad_kv_up = heads_finish(heads_back)
    last = last.astype(F32)
    small = jnp.sum(last[:, own_cols:], axis=0).reshape(-1)
    grad_down = both_halves(last[:, :own_cols], 1).reshape(-1, own_d)
    ffn_half = lax.optimization_barrier((ffn_half, last))[0]
    output = (hidden_one + both_halves(ffn_half, 0).astype(F32)).astype(BF16)
    edge = 2 * own_d + own_q
    edge_kv = edge + kv_gain.shape[0]
    return (
        output,
        grad_input,
        small[:own_d],
        jnp.transpose(grad_down[:qr]),
        small[2 * own_d : edge],
        grad_q_up,
        jnp.transpose(grad_down[qr:latents]),
        small[edge:edge_kv],
        grad_kv_up,
        grad_out_proj,
        small[own_d : 2 * own_d],
        jnp.transpose(small[edge_kv:].reshape(experts, own_d)),
        d_shared[0],
        d_shared[1],
        d_shared[2],
        grad_expert_gate,
        grad_expert_up,
        grad_expert_down,
    )


def solution(mesh):
    n, wt = mesh.devices.shape
    plane = math.gcd(4, n)
    mesh = jax.sharding.Mesh(
        mesh.devices.reshape(n // plane, plane, wt), CTX + ("wt",)
    )
    placed = (
        P(CTX, None),
        P(),
        P(CTX, None),
        P(CTX, None),
        P(CTX),
        P(CTX, None),
        P(CTX),
        P(CTX, "wt"),
        P(CTX, None),
        P(CTX),
        P(CTX, "wt"),
        P(CTX, "wt"),
        P(CTX),
        P(CTX, None),
        P(CTX, "wt"),
        P(CTX, "wt"),
        P(CTX, "wt"),
        P(CTX, None, "wt"),
        P(CTX, None, "wt"),
        P(CTX, "wt", None),
    )
    return jax.shard_map(
        layer,
        mesh=mesh,
        in_specs=placed,
        out_specs=(
            P(CTX, None),
            P(CTX, None),
            P(CTX),
            P(CTX, None),
            P(CTX),
            P(CTX, "wt"),
            P(CTX, None),
            P(CTX),
            P(CTX, "wt"),
            P(CTX, "wt"),
            P(CTX),
            P(CTX, None),
            P(CTX, "wt"),
            P(CTX, "wt"),
            P(CTX, "wt"),
            P(CTX, None, "wt"),
            P(CTX, None, "wt"),
            P(CTX, "wt", None),
        ),
        check_vma=False,
    )
```

```python
import math

import jax
import jax.numpy as jnp
from jax import lax
from jax.sharding import PartitionSpec as P


NOPE = 128
ROPE = 64
VDIM = 128
BLOCK = 64

rms_epsilon = 1e-06
rope_base = 50000.0
route_scale = 2.446


F32 = jnp.float32
BF16 = jnp.bfloat16


def dot(left_mat, right_mat):
    return lax.dot_general(
        left_mat, right_mat, (((1,), (0,)), ((), ())), preferred_element_type=F32
    )


def dot_rows(left_mat, right_mat):
    return lax.dot_general(
        left_mat, right_mat, (((1,), (1,)), ((), ())), preferred_element_type=F32
    )


def dot_cols(left_mat, right_mat):
    return lax.dot_general(
        left_mat, right_mat, (((0,), (0,)), ((), ())), preferred_element_type=F32
    )


def normalize(values, weights):
    inverse = lax.rsqrt(jnp.mean(values * values, axis=-1, keepdims=True) + rms_epsilon)
    return (values * inverse * weights, inverse)


def norm_backward(upstream, values, inverse, weights):
    unit_rows = values * inverse
    scaled = upstream * weights
    inner_mean = jnp.mean(scaled * unit_rows, axis=-1, keepdims=True)
    return (inverse * (scaled - unit_rows * inner_mean), jnp.sum(upstream * unit_rows, axis=0))


def rope_tables(positions):
    half_dim = ROPE // 2
    exponent = jnp.arange(half_dim, dtype=F32) * (2.0 / ROPE)
    frequency = jnp.exp(-exponent * math.log(rope_base))
    angles = positions.astype(F32)[:, None] * frequency[None, :]
    return (jnp.cos(angles), jnp.sin(angles))


def rotate(values, cosine, sine_part):
    half_dim = values.shape[-1] // 2
    first_half = values[..., :half_dim]
    second_half = values[..., half_dim:]
    return jnp.concatenate(
        [
            first_half * cosine - second_half * sine_part,
            first_half * sine_part + second_half * cosine,
        ],
        axis=-1,
    )


def unrotate(values, cosine, sine_part):
    return rotate(values, cosine, -sine_part)


def silu_parts(values):
    sigma = jax.nn.sigmoid(values)
    return (values * sigma, sigma * (1.0 + values * (1.0 - sigma)))


def positions_of(table_rows):
    offsets = jnp.arange(BLOCK, dtype=jnp.int32)
    return (table_rows[:, :, None] * BLOCK + offsets[None, None, :]).reshape(-1)


CTX = ("line", "plane")


def exchange(blocks, axes=CTX):
    return lax.all_to_all(blocks, axes, split_axis=0, concat_axis=0, tiled=True)


def wt_sum(values):
    return values + other_wt(values)


def other_wt(values):
    return lax.ppermute(values, "wt", [(0, 1), (1, 0)])


def layer(
    layer_input,
    block_table,
    routes,
    grad_output,
    norm1_gain,
    query_down_weight,
    q_gain,
    q_up,
    kv_down,
    kv_gain,
    kv_up,
    out_proj,
    norm2_gain,
    router,
    shared_gate,
    shared_up,
    shared_down,
    expert_gate,
    routed_expert_up_weight,
    expert_down,
):
    n = lax.axis_size(CTX)
    wt = lax.axis_size("wt")
    c = lax.axis_index(CTX)
    w = lax.axis_index("wt")
    rows, width = layer_input.shape
    tokens = n * rows
    kvr = kv_gain.shape[0] * n
    qr = q_gain.shape[0] * n
    head_dim = NOPE + ROPE
    heads = q_up.shape[1] // head_dim
    group = lax.axis_size("plane")
    groups = lax.axis_size("line")
    own_heads = heads // group
    g = lax.axis_index("plane")
    experts = router.shape[1]
    own_d = norm1_gain.shape[0]
    own_q = q_gain.shape[0]
    latents = qr + kvr + ROPE
    score_scale = head_dim ** (-0.5)

    def half_rows(values):
        size = values.shape[0] // wt
        return lax.dynamic_slice_in_dim(values, w * size, size, 0)

    def gather_rows(values):
        return lax.all_gather(half_rows(values), CTX + ("wt",), axis=0, tiled=True)

    def gather_tokens(mine):
        return lax.all_gather(mine, ("plane", "line", "wt"), axis=0, tiled=True)

    def wt_halves(left, right):
        theirs = other_wt(dot_cols(left, right[0]).astype(BF16))
        mine = lax.optimization_barrier(dot_cols(left, right[1]).astype(BF16))
        return mine + theirs

    def scatter_tokens(values, beside=()):
        some = lax.psum_scatter(values, "plane", scatter_dimension=0, tiled=True)
        some, beside = lax.optimization_barrier((some, beside))
        return lax.psum_scatter(some, "line", scatter_dimension=0, tiled=True), beside

    def both_halves(mine, axis):
        theirs = other_wt(mine)
        first, second = jnp.where(w == 0, mine, theirs), jnp.where(w == 0, theirs, mine)
        return jnp.concatenate([first, second], axis=axis)

    def group_moves(k):
        return [(i, i ^ k) for i in range(group)]

    def group_sum(values):
        cols = values.shape[1] // 2
        sent = lax.dynamic_slice_in_dim(values, (1 - w) * cols, cols, 1).astype(BF16)
        total = lax.dynamic_slice_in_dim(values, w * cols, cols, 1)
        total = (total + other_wt(sent).astype(F32)).reshape(group, rows, cols)
        own = lax.dynamic_index_in_dim(total, g, 0, keepdims=False)
        for k in range(1, group):
            block = lax.dynamic_index_in_dim(total, g ^ k, 0, keepdims=False).astype(BF16)
            own = own + lax.ppermute(block, "plane", group_moves(k)).astype(F32)
        return both_halves(own, 1)

    def group_gather(values):
        cols = values.shape[1] // 2
        mine = lax.dynamic_slice_in_dim(values, w * cols, cols, 1)
        out = jnp.zeros((group, rows, cols), values.dtype)
        out = lax.dynamic_update_index_in_dim(out, mine, g, 0)
        for k in range(1, group):
            got = lax.ppermute(mine, "plane", group_moves(k))
            out = lax.dynamic_update_index_in_dim(out, got, g ^ k, 0)
        return both_halves(out.reshape(group * rows, cols), 1)

    def own_group(values):
        start = lax.axis_index("line") * group * rows
        return lax.dynamic_slice_in_dim(values, start, group * rows, 0)

    lanes = 128

    def to_head_group(values):
        depth = values.shape[1] // group
        blocks = jnp.transpose(values.reshape(values.shape[0], group, depth), (1, 0, 2))
        blocks = jnp.broadcast_to(blocks[None], (groups,) + blocks.shape)
        return exchange(blocks.reshape((n,) + blocks.shape[2:])).reshape(-1, depth)

    lanes = 128

    def pack_heads(terms):
        packed = []
        for values in terms:
            k, depth = values.shape[0] // n, values.shape[1]
            split = values.astype(BF16).reshape(groups, group, k, depth // lanes, lanes)
            split = jnp.transpose(split, (0, 1, 3, 2, 4))
            packed.append(split.reshape(groups, group, -1, lanes))
        return jnp.concatenate(packed, axis=2).reshape(-1, lanes)

    def sum_packed(packed):
        summed = lax.psum_scatter(packed, "line", scatter_dimension=0, tiled=True)
        blocks = summed.reshape(group, -1, lanes)
        own = lax.dynamic_index_in_dim(blocks, g, 0, keepdims=False)
        out = lax.dynamic_update_index_in_dim(jnp.zeros_like(blocks), own, g, 0)
        for k in range(1, group):
            sent = lax.dynamic_index_in_dim(blocks, g ^ k, 0, keepdims=False)
            got = lax.ppermute(sent, "plane", group_moves(k))
            out = lax.dynamic_update_index_in_dim(out, got, g ^ k, 0)
        return out

    def unpack_heads(got, weights):
        out, at = [], 0
        for weight in weights:
            k, blocks = weight.shape[0], weight.shape[1] // group // lanes
            part = got[:, at : at + k * blocks].reshape(group, blocks, k, lanes)
            out.append(jnp.transpose(part, (2, 0, 1, 3)).reshape(k, -1).astype(F32))
            at += k * blocks
        return out

    gains = exchange(
        jnp.broadcast_to(
            jnp.concatenate([norm1_gain, norm2_gain, q_gain, kv_gain])[None],
            (n, 2 * own_d + q_gain.shape[0] + kv_gain.shape[0]),
        )
    )
    pad = -(latents + experts) % 128
    down_own = jnp.concatenate(
        [query_down_weight, kv_down, router, jnp.zeros((own_d, pad), BF16)], axis=1
    )
    if rows == own_d:
        gathered = (gather_rows(jnp.concatenate([layer_input, down_own], axis=1)),)
    else:
        gathered = (gather_rows(layer_input), gather_rows(down_own))
    ff_own = shared_gate.shape[1] // n
    shared_stack = jnp.stack([shared_gate, shared_up, shared_down], axis=0)
    shared_blocks = jnp.transpose(shared_stack.reshape(3, own_d, n, ff_own), (2, 0, 3, 1))
    gathered, kv_up_heads, q_up_heads, gains, late = lax.optimization_barrier(
        (
            gathered,
            to_head_group(kv_up),
            to_head_group(q_up),
            gains,
            (half_rows(grad_output), out_proj),
        )
    )
    go_half, out_late = late
    go_all = gather_tokens(go_half)
    out_heads = to_head_group(out_late)
    if rows == own_d:
        x_all, down_all = gathered[0][:, :width], gathered[0][:, width:]
    else:
        x_all, down_all = gathered
    q_down_all = down_all[:, :qr]
    kv_down_all = down_all[:, qr:latents]
    router_all = down_all[:, latents : latents + experts]
    norm1_full = gains[:, :own_d].reshape(-1).astype(F32)
    norm2_full = gains[:, own_d : 2 * own_d].reshape(-1).astype(F32)
    qgain_full = gains[:, 2 * own_d : 2 * own_d + own_q].reshape(-1).astype(F32)
    kvgain_full = gains[:, 2 * own_d + own_q :].reshape(-1).astype(F32)

    key_positions = positions_of(block_table)
    query_positions = own_group(key_positions)
    own_positions = positions_of(lax.dynamic_slice_in_dim(block_table, c, 1, 0))
    cosine_all, sine_all = rope_tables(key_positions)
    cosine_group, sine_group = rope_tables(query_positions)
    cosine, sine = rope_tables(own_positions)

    normed_all = lax.optimization_barrier(
        normalize(x_all.astype(F32), norm1_full)[0].astype(BF16)
    )
    kv_latent_all = dot(normed_all, kv_down_all)
    latent_all = normalize(kv_latent_all[:, :kvr], kvgain_full)[0].astype(BF16)
    rope_all = rotate(kv_latent_all[:, kvr:], cosine_all, sine_all).astype(BF16)
    q_normed_group = normalize(dot(own_group(normed_all), q_down_all), qgain_full)[0].astype(BF16)
    query_f = dot(q_normed_group, q_up_heads)
    key_values = dot(latent_all, kv_up_heads).astype(BF16)
    allowed = query_positions[:, None] >= key_positions[None, :]
    queries, keys, values_heads, exacts, attended = [], [], [], [], []
    for h in range(own_heads):
        query_h = query_f[:, h * head_dim : (h + 1) * head_dim]
        query_h = jnp.concatenate(
            [query_h[:, :NOPE], rotate(query_h[:, NOPE:], cosine_group, sine_group)], axis=-1
        ).astype(BF16)
        kv_h = key_values[:, h * (NOPE + VDIM) : (h + 1) * (NOPE + VDIM)]
        keys_h = jnp.concatenate([kv_h[:, :NOPE], rope_all], axis=-1)
        scores = dot_rows(query_h, keys_h) * score_scale
        log_total = jnp.log(
            jnp.sum(jnp.where(allowed, jnp.exp(scores), 0.0), axis=-1, keepdims=True)
        )
        exact = jnp.where(allowed, jnp.exp(scores - log_total), 0.0)
        queries.append(query_h)
        keys.append(keys_h)
        values_heads.append(kv_h[:, NOPE:])
        exacts.append(exact)
        attended.append(dot(exact.astype(BF16), kv_h[:, NOPE:]).astype(BF16))
    attention = jnp.concatenate(attended, axis=1)

    inputs = layer_input.astype(F32)
    hidden_one = inputs + group_sum(dot_rows(attention, out_heads))
    normed2_f, inverse_two = normalize(hidden_one, norm2_full)
    normed_two = normed2_f.astype(BF16)
    sigma = jax.nn.sigmoid(dot(normed_two, router_all))
    expert_ids = jnp.arange(experts, dtype=jnp.int32)
    picked = jnp.any(routes[..., None] == expert_ids[None, None, :], axis=1)
    chosen = jnp.where(picked, sigma, 0.0)
    chosen_total = jnp.sum(chosen, axis=-1, keepdims=True)
    gates = route_scale * chosen / chosen_total
    gates_high = gates.astype(BF16)
    gates_low = (gates - gates_high.astype(F32)).astype(BF16)
    gates_pad = jnp.zeros((rows, -2 * experts % 128), BF16)
    sent_rows = jnp.concatenate([normed_two, gates_high, gates_low, gates_pad], axis=1)
    sent_rows, go_all, shared_blocks = lax.optimization_barrier((sent_rows, go_all, shared_blocks))
    got_rows = gather_tokens(half_rows(sent_rows))

    e_gate, e_up = jnp.transpose(expert_gate[0]), jnp.transpose(routed_expert_up_weight[0])
    ff = e_gate.shape[0]
    ff_all = ff + ff_own
    shared_got = exchange(shared_blocks)
    s_gate, s_up, s_down = jnp.transpose(shared_got, (1, 2, 0, 3)).reshape(3, ff_own, width)
    mats = jnp.concatenate([e_gate, s_gate, e_up, s_up, expert_down[0], s_down], axis=0)
    back_unit = dot_rows(mats[2 * ff_all :], go_all)
    normed_f, inverse_one = normalize(inputs, norm1_full)
    normed = normed_f.astype(BF16)
    q_latent = dot(normed, q_down_all)
    q_inverse = normalize(q_latent, qgain_full)[1]
    kv_latent = dot(normed, kv_down_all)[:, :kvr]
    kv_inverse = normalize(kv_latent, kvgain_full)[1]
    normed_half = lax.dynamic_index_in_dim(
        normed_all.reshape(n, wt, rows // wt, width), w, 1, keepdims=False
    ).reshape(tokens // wt, width)
    cols = width // wt
    mats_theirs = lax.dynamic_slice_in_dim(mats, (1 - w) * cols, cols, 1)
    mats_mine = lax.dynamic_slice_in_dim(mats, w * cols, cols, 1)
    ready = (mats, back_unit, inverse_one, q_latent, q_inverse, kv_latent, kv_inverse, normed_half)
    got_rows, ready, mats_theirs, mats_mine = lax.optimization_barrier(
        (got_rows, ready, mats_theirs, mats_mine)
    )
    mats, back_unit, inverse_one, q_latent, q_inverse, kv_latent, kv_inverse, normed_half = ready
    normed_two_all = got_rows[:, :width]
    got_gates = got_rows[:, width : width + 2 * experts].astype(F32)
    is_own = (jnp.arange(2 * experts) % experts == c)[None]
    gate_own = jnp.sum(jnp.where(is_own, got_gates, 0.0), axis=-1)[None]

    gate_pre = dot_rows(mats[:ff_all], normed_two_all)
    up_pre = dot_rows(mats[ff_all : 2 * ff_all], normed_two_all)
    act, slope = silu_parts(gate_pre)
    hidden = act * up_pre
    is_expert = (jnp.arange(ff_all) < ff)[:, None]
    scale = jnp.where(is_expert, gate_own, 1.0)
    hidden_scaled = (hidden * scale).astype(BF16)
    back = back_unit * scale
    d_gate = (back * up_pre * slope).astype(BF16)
    d_up = (back * act).astype(BF16)
    grad_gate_own = jnp.sum(jnp.where(is_expert, back_unit * hidden, 0.0), axis=0)
    d_normed = wt_halves(
        jnp.concatenate([d_gate, d_up], axis=0),
        (mats_theirs[: 2 * ff_all], mats_mine[: 2 * ff_all]),
    )
    d_normed, grad_gate_own, d_gate, d_up, hidden_scaled = lax.optimization_barrier(
        (d_normed, grad_gate_own, d_gate, d_up, hidden_scaled)
    )
    ffn_part = wt_halves(hidden_scaled, (mats_theirs[2 * ff_all :], mats_mine[2 * ff_all :]))
    grad_expert_gate = dot(d_gate[:ff], normed_two_all)
    grad_expert_up = dot(d_up[:ff], normed_two_all)
    grad_expert_down = dot(hidden_scaled[:ff], go_all)
    grad_gates = wt_sum(grad_gate_own).reshape(group, groups, rows)
    grad_gates = exchange(jnp.transpose(grad_gates, (1, 0, 2)).reshape(n, rows))
    grad_expert_gate = jnp.transpose(grad_expert_gate)[None]
    grad_expert_up = jnp.transpose(grad_expert_up)[None]
    grad_expert_down = grad_expert_down[None]
    d_shared_in = dot(jnp.concatenate([d_gate[ff:], d_up[ff:]], axis=0), normed_two_all)
    d_shared_out = dot(hidden_scaled[ff:], go_all)
    d_shared = jnp.concatenate([d_shared_in, d_shared_out], axis=0).astype(BF16)
    d_shared = jnp.transpose(d_shared.reshape(3, ff_own, n, own_d), (2, 0, 1, 3))
    d_shared = exchange(d_shared)
    grad_normed_half, (d_shared, grad_gates, ffn_part, grad_expert_gate) = scatter_tokens(
        d_normed, (d_shared, grad_gates, ffn_part, grad_expert_gate)
    )
    grad_normed_half, ffn_part, grad_expert_up, grad_expert_down = lax.optimization_barrier(
        (grad_normed_half, ffn_part, grad_expert_up, grad_expert_down)
    )
    grad_normed_two = both_halves(grad_normed_half, 1).astype(F32)

    grad_gates = jnp.where(picked, jnp.transpose(grad_gates), 0.0)
    grad_chosen = (
        route_scale * grad_gates - jnp.sum(grad_gates * gates, axis=-1, keepdims=True)
    ) / chosen_total
    grad_logits = (grad_chosen * chosen * (1.0 - chosen)).astype(BF16)
    upstream = grad_output.astype(F32)
    grad_normed_two = grad_normed_two + dot_rows(grad_logits, router_all)
    grad_router_part = dot_cols(grad_logits, normed_two)
    grad_hidden, norm2_part = norm_backward(grad_normed_two, hidden_one, inverse_two, norm2_full)
    grad_hidden = grad_hidden + upstream
    grad_hidden_half = grad_hidden.astype(BF16)
    hidden_group = group_gather(grad_hidden_half)
    hidden_group, ffn_part = lax.optimization_barrier((hidden_group, ffn_part))
    ffn_half = scatter_tokens(ffn_part)[0]
    grad_attention = dot(hidden_group, out_heads).astype(BF16)

    query_parts, kv_parts, rope_part = [], [], 0.0
    for h in range(own_heads):
        grad_att = grad_attention[:, h * VDIM : (h + 1) * VDIM]
        delta = jnp.sum(grad_att.astype(F32) * attended[h].astype(F32), axis=-1, keepdims=True)
        grad_probs = dot_rows(grad_att, values_heads[h])
        grad_scores = (exacts[h] * (grad_probs - delta)).astype(BF16)
        grad_query = score_scale * dot(grad_scores, keys[h])
        grad_keys = score_scale * dot_cols(grad_scores, queries[h])
        grad_values = dot_cols(exacts[h].astype(BF16), grad_att)
        query_parts.append(grad_query[:, :NOPE])
        query_parts.append(unrotate(grad_query[:, NOPE:], cosine_group, sine_group))
        kv_parts.append(grad_keys[:, :NOPE])
        kv_parts.append(grad_values)
        rope_part = rope_part + grad_keys[:, NOPE:]
    grad_query_half = jnp.concatenate(query_parts, axis=-1).astype(BF16)
    grad_kv_heads = jnp.concatenate(kv_parts, axis=-1).astype(BF16)
    kv_part = jnp.concatenate([dot_rows(grad_kv_heads, kv_up_heads), rope_part], axis=1)
    kv_part = kv_part.astype(BF16).reshape(n, wt, rows // wt, kvr + ROPE)
    kv_theirs = other_wt(lax.dynamic_index_in_dim(kv_part, 1 - w, 1, keepdims=False))
    kv_part = lax.dynamic_index_in_dim(kv_part, w, 1, keepdims=False) + kv_theirs
    kv_got, grad_q_normed, packed = lax.optimization_barrier(
        (
            exchange(kv_part),
            group_sum(dot_rows(grad_query_half, q_up_heads)),
            pack_heads(
                (
                    dot_cols(hidden_group, attention),
                    dot_cols(q_normed_group, grad_query_half),
                    dot_cols(latent_all, grad_kv_heads),
                )
            ),
        )
    )
    kv_own = both_halves(jnp.sum(kv_got.astype(F32), axis=0), 0)
    heads_back = sum_packed(packed)
    d_shared = jnp.transpose(d_shared, (1, 3, 0, 2)).reshape(3, own_d, n * ff_own).astype(F32)

    grad_q_latent, qgain_part = norm_backward(grad_q_normed, q_latent, q_inverse, qgain_full)
    grad_kv_part, kvgain_part = norm_backward(
        kv_own[:, :kvr], kv_latent, kv_inverse, kvgain_full
    )
    grad_rope_raw = unrotate(kv_own[:, kvr:], cosine, sine)
    grad_latents = jnp.concatenate([grad_q_latent, grad_kv_part, grad_rope_raw], axis=-1).astype(
        BF16
    )
    own_cols = -(-latents // (8 * n * wt)) * 8
    col_blocks = jnp.pad(half_rows(grad_latents), ((0, 0), (0, own_cols * n * wt - latents)))
    col_blocks = jnp.transpose(col_blocks.reshape(rows // wt, n, wt * own_cols), (1, 0, 2))
    latent_cols = exchange(col_blocks)
    grad_normed = dot_rows(grad_latents, down_all[:, :latents])
    grad_input, norm1_part = norm_backward(grad_normed, inputs, inverse_one, norm1_full)
    grad_input = grad_input + grad_hidden
    latent_cols, grad_input, norm1_part, d_shared = lax.optimization_barrier(
        (latent_cols, grad_input, norm1_part, d_shared)
    )
    latent_cols = latent_cols.reshape(tokens // wt, wt * own_cols)
    down_cols = dot_cols(latent_cols, normed_half)
    down_theirs = other_wt(lax.dynamic_slice_in_dim(down_cols, (1 - w) * own_cols, own_cols, 0))
    down_cols = lax.dynamic_slice_in_dim(down_cols, w * own_cols, own_cols, 0) + down_theirs
    down_cols = jnp.transpose(down_cols.reshape(own_cols, n, own_d), (1, 0, 2))

    small = jnp.concatenate(
        [
            norm1_part.reshape(n, -1),
            norm2_part.reshape(n, -1),
            qgain_part.reshape(n, -1),
            kvgain_part.reshape(n, -1),
            jnp.transpose(grad_router_part.reshape(experts, n, own_d), (1, 0, 2)).reshape(n, -1),
        ],
        axis=1,
    )
    last = jnp.concatenate([down_cols, small.reshape(n, -1, own_d)], axis=1)
    last = exchange(last.astype(BF16))
    grad_out_proj, grad_q_up, grad_kv_up = unpack_heads(heads_back, (out_proj, q_up, kv_up))
    small = jnp.sum(last[:, own_cols:].astype(F32), axis=0).reshape(-1)
    grad_down = both_halves(last[:, :own_cols], 1).reshape(-1, own_d).astype(F32)
    ffn_half = lax.optimization_barrier((ffn_half, last))[0]
    output = (hidden_one + both_halves(ffn_half, 1).astype(F32)).astype(BF16)
    edge = 2 * own_d + own_q
    edge_kv = edge + kv_gain.shape[0]
    return (
        output,
        grad_input,
        small[:own_d],
        jnp.transpose(grad_down[:qr]),
        small[2 * own_d : edge],
        grad_q_up,
        jnp.transpose(grad_down[qr:latents]),
        small[edge:edge_kv],
        grad_kv_up,
        grad_out_proj,
        small[own_d : 2 * own_d],
        jnp.transpose(small[edge_kv:].reshape(experts, own_d)),
        d_shared[0],
        d_shared[1],
        d_shared[2],
        grad_expert_gate,
        grad_expert_up,
        grad_expert_down,
    )


def solution(mesh):
    n, wt = mesh.devices.shape
    plane = math.gcd(4, n)
    mesh = jax.sharding.Mesh(
        mesh.devices.reshape(n // plane, plane, wt), CTX + ("wt",)
    )
    placed = (
        P(CTX, None),
        P(),
        P(CTX, None),
        P(CTX, None),
        P(CTX),
        P(CTX, None),
        P(CTX),
        P(CTX, "wt"),
        P(CTX, None),
        P(CTX),
        P(CTX, "wt"),
        P(CTX, "wt"),
        P(CTX),
        P(CTX, None),
        P(CTX, "wt"),
        P(CTX, "wt"),
        P(CTX, "wt"),
        P(CTX, None, "wt"),
        P(CTX, None, "wt"),
        P(CTX, "wt", None),
    )
    return jax.shard_map(
        layer,
        mesh=mesh,
        in_specs=placed,
        out_specs=(
            P(CTX, None),
            P(CTX, None),
            P(CTX),
            P(CTX, None),
            P(CTX),
            P(CTX, "wt"),
            P(CTX, None),
            P(CTX),
            P(CTX, "wt"),
            P(CTX, "wt"),
            P(CTX),
            P(CTX, None),
            P(CTX, "wt"),
            P(CTX, "wt"),
            P(CTX, "wt"),
            P(CTX, None, "wt"),
            P(CTX, None, "wt"),
            P(CTX, "wt", None),
        ),
        check_vma=False,
    )
```

```python
import math

import jax
import jax.numpy as jnp
from jax import lax
from jax.experimental import pallas as pl
from jax.experimental.pallas import tpu as pltpu
from jax.sharding import PartitionSpec as P


NOPE = 128
ROPE = 64
VDIM = 128
BLOCK = 64

rms_epsilon = 1e-06
rope_base = 50000.0
route_scale = 2.446


F32 = jnp.float32
BF16 = jnp.bfloat16


def dot(left_mat, right_mat):
    return lax.dot_general(
        left_mat, right_mat, (((1,), (0,)), ((), ())), preferred_element_type=F32
    )


def dot_rows(left_mat, right_mat):
    return lax.dot_general(
        left_mat, right_mat, (((1,), (1,)), ((), ())), preferred_element_type=F32
    )


def dot_cols(left_mat, right_mat):
    return lax.dot_general(
        left_mat, right_mat, (((0,), (0,)), ((), ())), preferred_element_type=F32
    )


def normalize(values, weights):
    inverse = lax.rsqrt(jnp.mean(values * values, axis=-1, keepdims=True) + rms_epsilon)
    return (values * inverse * weights, inverse)


def norm_backward(upstream, values, inverse, weights):
    unit_rows = values * inverse
    scaled = upstream * weights
    inner_mean = jnp.mean(scaled * unit_rows, axis=-1, keepdims=True)
    return (inverse * (scaled - unit_rows * inner_mean), jnp.sum(upstream * unit_rows, axis=0))


def rope_tables(positions):
    half_dim = ROPE // 2
    exponent = jnp.arange(half_dim, dtype=F32) * (2.0 / ROPE)
    frequency = jnp.exp(-exponent * math.log(rope_base))
    angles = positions.astype(F32)[:, None] * frequency[None, :]
    return (jnp.cos(angles), jnp.sin(angles))


def rotate(values, cosine, sine_part):
    half_dim = values.shape[-1] // 2
    first_half = values[..., :half_dim]
    second_half = values[..., half_dim:]
    return jnp.concatenate(
        [
            first_half * cosine - second_half * sine_part,
            first_half * sine_part + second_half * cosine,
        ],
        axis=-1,
    )


def unrotate(values, cosine, sine_part):
    return rotate(values, cosine, -sine_part)


def silu_parts(values):
    sigma = jax.nn.sigmoid(values)
    return (values * sigma, sigma * (1.0 + values * (1.0 - sigma)))


def positions_of(table_rows):
    offsets = jnp.arange(BLOCK, dtype=jnp.int32)
    return (table_rows[:, :, None] * BLOCK + offsets[None, None, :]).reshape(-1)


CTX = ("line", "plane")


def exchange(blocks, axes=CTX):
    return lax.all_to_all(blocks, axes, split_axis=0, concat_axis=0, tiled=True)


def wt_sum(values):
    return values + other_wt(values)


def other_wt(values):
    return lax.ppermute(values, "wt", [(0, 1), (1, 0)])


def latents_back(grad_q, q_latent, q_gain, grad_kv, kv_latent, kv_gain, rest):
    rows, qr = q_latent.shape
    kvr, extra = kv_latent.shape[1], rest.shape[1]

    def kernel(gq_ref, q_ref, qw_ref, gk_ref, k_ref, kw_ref, rest_ref, out_ref, qg_ref, kg_ref):
        def back(upstream, values, weights):
            inverse = lax.rsqrt(jnp.mean(values * values, axis=-1, keepdims=True) + rms_epsilon)
            unit_rows = values * inverse
            scaled = upstream * weights
            inner_mean = jnp.mean(scaled * unit_rows, axis=-1, keepdims=True)
            gain = jnp.sum(upstream * unit_rows, axis=0, keepdims=True)
            return inverse * (scaled - unit_rows * inner_mean), gain

        part, qg_ref[...] = back(gq_ref[...], q_ref[...], qw_ref[...])
        out_ref[:, :qr] = part.astype(BF16)
        part, kg_ref[...] = back(gk_ref[...], k_ref[...], kw_ref[...])
        out_ref[:, qr : qr + kvr] = part.astype(BF16)
        out_ref[:, qr + kvr :] = rest_ref[...].astype(BF16)

    return pl.pallas_call(
        kernel,
        out_shape=(
            jax.ShapeDtypeStruct((rows, qr + kvr + extra), BF16),
            jax.ShapeDtypeStruct((1, qr), F32),
            jax.ShapeDtypeStruct((1, kvr), F32),
        ),
        cost_estimate=pl.CostEstimate(
            flops=20 * rows * (qr + kvr), bytes_accessed=12 * rows * (qr + kvr), transcendentals=0
        ),
        name="latents_back",
    )(grad_q, q_latent, q_gain.reshape(1, qr), grad_kv, kv_latent, kv_gain.reshape(1, kvr), rest)


def expert_rows(rows_in, gate_mat, up_mat, back_unit, gate_row, experts_ff):
    units, width = gate_mat.shape
    tokens = rows_in.shape[0]
    tile = 256

    def kernel(rows_ref, gate_mat_ref, up_mat_ref, back_ref, gate_ref, h_ref, d_ref, gg_ref):
        rows = rows_ref[...]
        gate_pre = dot_rows(gate_mat_ref[...], rows)
        up_pre = dot_rows(up_mat_ref[...], rows)
        act, slope = silu_parts(gate_pre)
        hidden = act * up_pre
        unit = lax.broadcasted_iota(jnp.int32, (units, tile), 0)
        is_expert = unit < experts_ff
        scale = jnp.where(is_expert, jnp.broadcast_to(gate_ref[...], (units, tile)), 1.0)
        back = back_ref[...]
        gg_ref[...] = jnp.sum(jnp.where(is_expert, back * hidden, 0.0), axis=0, keepdims=True)
        h_ref[...] = (hidden * scale).astype(BF16)
        back = back * scale
        d_ref[0] = (back * up_pre * slope).astype(BF16)
        d_ref[1] = (back * act).astype(BF16)

    by_tile = pl.BlockSpec((units, tile), lambda i: (0, i))
    fixed = pl.BlockSpec((units, width), lambda i: (0, 0), pipeline_mode=pl.Buffered(1))
    row = pl.BlockSpec((1, tile), lambda i: (0, i))
    return pl.pallas_call(
        kernel,
        grid=(tokens // tile,),
        in_specs=[pl.BlockSpec((tile, width), lambda i: (i, 0)), fixed, fixed, by_tile, row],
        out_specs=[by_tile, pl.BlockSpec((2, units, tile), lambda i: (0, 0, i)), row],
        out_shape=(
            jax.ShapeDtypeStruct((units, tokens), BF16),
            jax.ShapeDtypeStruct((2, units, tokens), BF16),
            jax.ShapeDtypeStruct((1, tokens), F32),
        ),
        compiler_params=pltpu.CompilerParams(vmem_limit_bytes=48 * 1024 * 1024),
        cost_estimate=pl.CostEstimate(
            flops=4 * units * width * tokens,
            bytes_accessed=2 * tokens * width + 4 * units * width + 10 * units * tokens,
            transcendentals=units * tokens,
        ),
        name="expert_rows",
    )(rows_in, gate_mat, up_mat, back_unit, gate_row)


def layer(
    layer_input,
    block_table,
    routes,
    grad_output,
    norm1_gain,
    query_down_weight,
    q_gain,
    q_up,
    kv_down,
    kv_gain,
    kv_up,
    out_proj,
    norm2_gain,
    router,
    shared_gate,
    shared_up,
    shared_down,
    expert_gate,
    routed_expert_up_weight,
    expert_down,
):
    n = lax.axis_size(CTX)
    wt = lax.axis_size("wt")
    c = lax.axis_index(CTX)
    w = lax.axis_index("wt")
    rows, width = layer_input.shape
    tokens = n * rows
    kvr = kv_gain.shape[0] * n
    qr = q_gain.shape[0] * n
    head_dim = NOPE + ROPE
    heads = q_up.shape[1] // head_dim
    group = lax.axis_size("plane")
    groups = lax.axis_size("line")
    own_heads = heads // group
    g = lax.axis_index("plane")
    experts = router.shape[1]
    own_d = norm1_gain.shape[0]
    own_q = q_gain.shape[0]
    latents = qr + kvr + ROPE
    score_scale = head_dim ** (-0.5)

    def half_rows(values):
        size = values.shape[0] // wt
        return lax.dynamic_slice_in_dim(values, w * size, size, 0)

    def gather_rows(values):
        return lax.all_gather(half_rows(values), CTX + ("wt",), axis=0, tiled=True)

    def gather_tokens(mine):
        return lax.all_gather(mine, ("plane", "line", "wt"), axis=0, tiled=True)

    def wt_halves(left, right):
        theirs = other_wt(dot_cols(left, right[0]).astype(BF16))
        mine = lax.optimization_barrier(dot_cols(left, right[1]).astype(BF16))
        return mine + theirs

    def scatter_tokens(values, beside=()):
        some = lax.psum_scatter(values, "plane", scatter_dimension=0, tiled=True)
        some, beside = lax.optimization_barrier((some, beside))
        return lax.psum_scatter(some, "line", scatter_dimension=0, tiled=True), beside

    def both_halves(mine, axis):
        theirs = other_wt(mine)
        first, second = jnp.where(w == 0, mine, theirs), jnp.where(w == 0, theirs, mine)
        return jnp.concatenate([first, second], axis=axis)

    def group_moves(k):
        return [(i, i ^ k) for i in range(group)]

    def group_sum(values):
        cols = values.shape[1] // 2
        sent = lax.dynamic_slice_in_dim(values, (1 - w) * cols, cols, 1).astype(BF16)
        total = lax.dynamic_slice_in_dim(values, w * cols, cols, 1)
        total = (total + other_wt(sent).astype(F32)).reshape(group, rows, cols)
        own = lax.dynamic_index_in_dim(total, g, 0, keepdims=False)
        for k in range(1, group):
            block = lax.dynamic_index_in_dim(total, g ^ k, 0, keepdims=False).astype(BF16)
            own = own + lax.ppermute(block, "plane", group_moves(k)).astype(F32)
        return both_halves(own, 1)

    def group_gather(values):
        cols = values.shape[1] // 2
        mine = lax.dynamic_slice_in_dim(values, w * cols, cols, 1)
        out = jnp.zeros((group, rows, cols), values.dtype)
        out = lax.dynamic_update_index_in_dim(out, mine, g, 0)
        for k in range(1, group):
            got = lax.ppermute(mine, "plane", group_moves(k))
            out = lax.dynamic_update_index_in_dim(out, got, g ^ k, 0)
        return both_halves(out.reshape(group * rows, cols), 1)

    def own_group(values):
        start = lax.axis_index("line") * group * rows
        return lax.dynamic_slice_in_dim(values, start, group * rows, 0)

    lanes = 128

    def to_head_group(values):
        depth = values.shape[1] // group
        blocks = jnp.transpose(values.reshape(values.shape[0], group, depth), (1, 0, 2))
        blocks = jnp.broadcast_to(blocks[None], (groups,) + blocks.shape)
        return exchange(blocks.reshape((n,) + blocks.shape[2:])).reshape(-1, depth)

    lanes = 128

    def pack_heads(terms):
        packed = []
        for values in terms:
            k, depth = values.shape[0] // n, values.shape[1]
            split = values.astype(BF16).reshape(groups, group, k, depth // lanes, lanes)
            split = jnp.transpose(split, (0, 1, 3, 2, 4))
            packed.append(split.reshape(groups, group, -1, lanes))
        return jnp.concatenate(packed, axis=2).reshape(-1, lanes)

    def sum_packed(packed):
        summed = lax.psum_scatter(packed, "line", scatter_dimension=0, tiled=True)
        blocks = summed.reshape(group, -1, lanes)
        own = lax.dynamic_index_in_dim(blocks, g, 0, keepdims=False)
        out = lax.dynamic_update_index_in_dim(jnp.zeros_like(blocks), own, g, 0)
        for k in range(1, group):
            sent = lax.dynamic_index_in_dim(blocks, g ^ k, 0, keepdims=False)
            got = lax.ppermute(sent, "plane", group_moves(k))
            out = lax.dynamic_update_index_in_dim(out, got, g ^ k, 0)
        return out

    def unpack_heads(got, weights):
        out, at = [], 0
        for weight in weights:
            k, blocks = weight.shape[0], weight.shape[1] // group // lanes
            part = got[:, at : at + k * blocks].reshape(group, blocks, k, lanes)
            out.append(jnp.transpose(part, (2, 0, 1, 3)).reshape(k, -1).astype(F32))
            at += k * blocks
        return out

    gains = exchange(
        jnp.broadcast_to(
            jnp.concatenate([norm1_gain, norm2_gain, q_gain, kv_gain])[None],
            (n, 2 * own_d + q_gain.shape[0] + kv_gain.shape[0]),
        )
    )
    pad = -(latents + experts) % 128
    down_own = jnp.concatenate(
        [query_down_weight, kv_down, router, jnp.zeros((own_d, pad), BF16)], axis=1
    )
    if rows == own_d:
        gathered = (gather_rows(jnp.concatenate([layer_input, down_own], axis=1)),)
    else:
        gathered = (gather_rows(layer_input), gather_rows(down_own))
    ff_own = shared_gate.shape[1] // n
    shared_stack = jnp.stack([shared_gate, shared_up, shared_down], axis=0)
    shared_blocks = jnp.transpose(shared_stack.reshape(3, own_d, n, ff_own), (2, 0, 3, 1))
    gathered, kv_up_heads, q_up_heads, gains, late = lax.optimization_barrier(
        (
            gathered,
            to_head_group(kv_up),
            to_head_group(q_up),
            gains,
            (half_rows(grad_output), out_proj),
        )
    )
    go_half, out_late = late
    go_all = gather_tokens(go_half)
    out_heads = to_head_group(out_late)
    if rows == own_d:
        x_all, down_all = gathered[0][:, :width], gathered[0][:, width:]
    else:
        x_all, down_all = gathered
    q_down_all = down_all[:, :qr]
    kv_down_all = down_all[:, qr:latents]
    router_all = down_all[:, latents : latents + experts]
    norm1_full = gains[:, :own_d].reshape(-1).astype(F32)
    norm2_full = gains[:, own_d : 2 * own_d].reshape(-1).astype(F32)
    qgain_full = gains[:, 2 * own_d : 2 * own_d + own_q].reshape(-1).astype(F32)
    kvgain_full = gains[:, 2 * own_d + own_q :].reshape(-1).astype(F32)

    key_positions = positions_of(block_table)
    query_positions = own_group(key_positions)
    own_positions = positions_of(lax.dynamic_slice_in_dim(block_table, c, 1, 0))
    cosine_all, sine_all = rope_tables(key_positions)
    cosine_group, sine_group = rope_tables(query_positions)
    cosine, sine = rope_tables(own_positions)

    normed_all = lax.optimization_barrier(
        normalize(x_all.astype(F32), norm1_full)[0].astype(BF16)
    )
    kv_latent_all = dot(normed_all, kv_down_all)
    latent_all = normalize(kv_latent_all[:, :kvr], kvgain_full)[0].astype(BF16)
    rope_all = rotate(kv_latent_all[:, kvr:], cosine_all, sine_all).astype(BF16)
    q_normed_group = normalize(dot(own_group(normed_all), q_down_all), qgain_full)[0].astype(BF16)
    query_f = dot(q_normed_group, q_up_heads)
    key_values = dot(latent_all, kv_up_heads).astype(BF16)
    allowed = query_positions[:, None] >= key_positions[None, :]
    queries, keys, values_heads, exacts, attended = [], [], [], [], []
    for h in range(own_heads):
        query_h = query_f[:, h * head_dim : (h + 1) * head_dim]
        query_h = jnp.concatenate(
            [query_h[:, :NOPE], rotate(query_h[:, NOPE:], cosine_group, sine_group)], axis=-1
        ).astype(BF16)
        kv_h = key_values[:, h * (NOPE + VDIM) : (h + 1) * (NOPE + VDIM)]
        keys_h = jnp.concatenate([kv_h[:, :NOPE], rope_all], axis=-1)
        scores = dot_rows(query_h, keys_h) * score_scale
        log_total = jnp.log(
            jnp.sum(jnp.where(allowed, jnp.exp(scores), 0.0), axis=-1, keepdims=True)
        )
        exact = jnp.where(allowed, jnp.exp(scores - log_total), 0.0)
        queries.append(query_h)
        keys.append(keys_h)
        values_heads.append(kv_h[:, NOPE:])
        exacts.append(exact)
        attended.append(dot(exact.astype(BF16), kv_h[:, NOPE:]).astype(BF16))
    attention = jnp.concatenate(attended, axis=1)

    inputs = layer_input.astype(F32)
    hidden_one = inputs + group_sum(dot_rows(attention, out_heads))
    normed2_f, inverse_two = normalize(hidden_one, norm2_full)
    normed_two = normed2_f.astype(BF16)
    sigma = jax.nn.sigmoid(dot(normed_two, router_all))
    expert_ids = jnp.arange(experts, dtype=jnp.int32)
    picked = jnp.any(routes[..., None] == expert_ids[None, None, :], axis=1)
    chosen = jnp.where(picked, sigma, 0.0)
    chosen_total = jnp.sum(chosen, axis=-1, keepdims=True)
    gates = route_scale * chosen / chosen_total
    gates_high = gates.astype(BF16)
    gates_low = (gates - gates_high.astype(F32)).astype(BF16)
    gates_pad = jnp.zeros((rows, -2 * experts % 128), BF16)
    sent_rows = jnp.concatenate([normed_two, gates_high, gates_low, gates_pad], axis=1)
    sent_rows, go_all, shared_blocks = lax.optimization_barrier((sent_rows, go_all, shared_blocks))
    got_rows = gather_tokens(half_rows(sent_rows))

    e_gate, e_up = jnp.transpose(expert_gate[0]), jnp.transpose(routed_expert_up_weight[0])
    ff = e_gate.shape[0]
    ff_all = ff + ff_own
    shared_got = exchange(shared_blocks)
    s_gate, s_up, s_down = jnp.transpose(shared_got, (1, 2, 0, 3)).reshape(3, ff_own, width)
    gate_mat = jnp.concatenate([e_gate, s_gate], axis=0)
    up_mat = jnp.concatenate([e_up, s_up], axis=0)
    down_mat = jnp.concatenate([expert_down[0], s_down], axis=0)
    mats = jnp.concatenate([gate_mat, up_mat, down_mat], axis=0)
    back_unit = dot_rows(down_mat, go_all)
    normed_f, inverse_one = normalize(inputs, norm1_full)
    normed = normed_f.astype(BF16)
    q_latent = dot(normed, q_down_all)
    kv_latent = dot(normed, kv_down_all)[:, :kvr]
    normed_half = lax.dynamic_index_in_dim(
        normed_all.reshape(n, wt, rows // wt, width), w, 1, keepdims=False
    ).reshape(tokens // wt, width)
    cols = width // wt
    mats_theirs = lax.dynamic_slice_in_dim(mats, (1 - w) * cols, cols, 1)
    mats_mine = lax.dynamic_slice_in_dim(mats, w * cols, cols, 1)
    ready = (gate_mat, up_mat, back_unit, inverse_one, q_latent, kv_latent, normed_half)
    got_rows, ready, mats_theirs, mats_mine = lax.optimization_barrier(
        (got_rows, ready, mats_theirs, mats_mine)
    )
    gate_mat, up_mat, back_unit, inverse_one, q_latent, kv_latent, normed_half = ready
    normed_two_all = got_rows[:, :width]
    got_gates = got_rows[:, width : width + 2 * experts].astype(F32)
    is_own = (jnp.arange(2 * experts) % experts == c)[None]
    gate_own = jnp.sum(jnp.where(is_own, got_gates, 0.0), axis=-1)[None]

    hidden_scaled, d_pre, grad_gate_own = expert_rows(
        got_rows, gate_mat, up_mat, back_unit, gate_own, ff
    )
    grad_gate_own = grad_gate_own.reshape(tokens)
    d_normed = wt_halves(
        d_pre.reshape(2 * ff_all, tokens),
        (mats_theirs[: 2 * ff_all], mats_mine[: 2 * ff_all]),
    )
    d_normed, grad_gate_own, d_pre, hidden_scaled = lax.optimization_barrier(
        (d_normed, grad_gate_own, d_pre, hidden_scaled)
    )
    ffn_part = wt_halves(hidden_scaled, (mats_theirs[2 * ff_all :], mats_mine[2 * ff_all :]))
    grad_expert_gate = dot(d_pre[0, :ff], normed_two_all)
    grad_expert_up = dot(d_pre[1, :ff], normed_two_all)
    grad_expert_down = dot(hidden_scaled[:ff], go_all)
    grad_gates = wt_sum(grad_gate_own).reshape(group, groups, rows)
    grad_gates = exchange(jnp.transpose(grad_gates, (1, 0, 2)).reshape(n, rows))
    grad_expert_gate = jnp.transpose(grad_expert_gate)[None]
    grad_expert_up = jnp.transpose(grad_expert_up)[None]
    grad_expert_down = grad_expert_down[None]
    d_shared_in = dot(d_pre[:, ff:].reshape(2 * ff_own, tokens), normed_two_all)
    d_shared_out = dot(hidden_scaled[ff:], go_all)
    d_shared = jnp.concatenate([d_shared_in, d_shared_out], axis=0).astype(BF16)
    d_shared = jnp.transpose(d_shared.reshape(3, ff_own, n, own_d), (2, 0, 1, 3))
    d_shared = exchange(d_shared)
    grad_normed_half, (d_shared, grad_gates, ffn_part, grad_expert_gate) = scatter_tokens(
        d_normed, (d_shared, grad_gates, ffn_part, grad_expert_gate)
    )
    grad_normed_half, ffn_part, grad_expert_up, grad_expert_down = lax.optimization_barrier(
        (grad_normed_half, ffn_part, grad_expert_up, grad_expert_down)
    )
    grad_normed_two = both_halves(grad_normed_half, 1).astype(F32)

    grad_gates = jnp.where(picked, jnp.transpose(grad_gates), 0.0)
    grad_chosen = (
        route_scale * grad_gates - jnp.sum(grad_gates * gates, axis=-1, keepdims=True)
    ) / chosen_total
    grad_logits = (grad_chosen * chosen * (1.0 - chosen)).astype(BF16)
    upstream = grad_output.astype(F32)
    grad_normed_two = grad_normed_two + dot_rows(grad_logits, router_all)
    grad_router_part = dot_cols(grad_logits, normed_two)
    grad_hidden, norm2_part = norm_backward(grad_normed_two, hidden_one, inverse_two, norm2_full)
    grad_hidden = grad_hidden + upstream
    grad_hidden_half = grad_hidden.astype(BF16)
    hidden_group = group_gather(grad_hidden_half)
    ffn_half = scatter_tokens(ffn_part)[0]
    grad_attention = dot(hidden_group, out_heads).astype(BF16)

    query_parts, kv_parts, rope_part = [], [], 0.0
    for h in range(own_heads):
        grad_att = grad_attention[:, h * VDIM : (h + 1) * VDIM]
        delta = jnp.sum(grad_att.astype(F32) * attended[h].astype(F32), axis=-1, keepdims=True)
        grad_probs = dot_rows(grad_att, values_heads[h])
        grad_scores = (exacts[h] * (grad_probs - delta)).astype(BF16)
        grad_query = score_scale * dot(grad_scores, keys[h])
        grad_keys = score_scale * dot_cols(grad_scores, queries[h])
        grad_values = dot_cols(exacts[h].astype(BF16), grad_att)
        query_parts.append(grad_query[:, :NOPE])
        query_parts.append(unrotate(grad_query[:, NOPE:], cosine_group, sine_group))
        kv_parts.append(grad_keys[:, :NOPE])
        kv_parts.append(grad_values)
        rope_part = rope_part + grad_keys[:, NOPE:]
    grad_query_half = jnp.concatenate(query_parts, axis=-1).astype(BF16)
    grad_kv_heads = jnp.concatenate(kv_parts, axis=-1).astype(BF16)
    kv_part = jnp.concatenate([dot_rows(grad_kv_heads, kv_up_heads), rope_part], axis=1)
    kv_part = kv_part.astype(BF16).reshape(n, wt, rows // wt, kvr + ROPE)
    kv_theirs = other_wt(lax.dynamic_index_in_dim(kv_part, 1 - w, 1, keepdims=False))
    kv_part = lax.dynamic_index_in_dim(kv_part, w, 1, keepdims=False) + kv_theirs
    kv_got, grad_q_normed, packed = lax.optimization_barrier(
        (
            exchange(kv_part),
            group_sum(dot_rows(grad_query_half, q_up_heads)),
            pack_heads(
                (
                    dot_cols(hidden_group, attention),
                    dot_cols(q_normed_group, grad_query_half),
                    dot_cols(latent_all, grad_kv_heads),
                )
            ),
        )
    )
    kv_own = both_halves(jnp.sum(kv_got.astype(F32), axis=0), 0)
    heads_back = sum_packed(packed)
    d_shared = jnp.transpose(d_shared, (1, 3, 0, 2)).reshape(3, own_d, n * ff_own).astype(F32)

    own_cols = -(-latents // (8 * n * wt)) * 8
    grad_rope_raw = unrotate(kv_own[:, kvr:], cosine, sine)
    rest = jnp.pad(grad_rope_raw, ((0, 0), (0, own_cols * n * wt - latents)))
    grad_latents, qgain_part, kvgain_part = latents_back(
        grad_q_normed, q_latent, qgain_full, kv_own[:, :kvr], kv_latent, kvgain_full, rest
    )
    col_blocks = half_rows(grad_latents)
    col_blocks = jnp.transpose(col_blocks.reshape(rows // wt, n, wt * own_cols), (1, 0, 2))
    latent_cols = exchange(col_blocks)
    grad_normed = dot_rows(grad_latents[:, :latents], down_all[:, :latents])
    grad_input, norm1_part = norm_backward(grad_normed, inputs, inverse_one, norm1_full)
    grad_input = grad_input + grad_hidden
    latent_cols, grad_input, norm1_part, d_shared = lax.optimization_barrier(
        (latent_cols, grad_input, norm1_part, d_shared)
    )
    latent_cols = latent_cols.reshape(tokens // wt, wt * own_cols)
    down_cols = dot_cols(latent_cols, normed_half)
    down_theirs = other_wt(lax.dynamic_slice_in_dim(down_cols, (1 - w) * own_cols, own_cols, 0))
    down_cols = lax.dynamic_slice_in_dim(down_cols, w * own_cols, own_cols, 0) + down_theirs
    down_cols = jnp.transpose(down_cols.reshape(own_cols, n, own_d), (1, 0, 2))

    small = jnp.concatenate(
        [
            norm1_part.reshape(n, -1),
            norm2_part.reshape(n, -1),
            qgain_part.reshape(n, -1),
            kvgain_part.reshape(n, -1),
            jnp.transpose(grad_router_part.reshape(experts, n, own_d), (1, 0, 2)).reshape(n, -1),
        ],
        axis=1,
    )
    last = jnp.concatenate([down_cols, small.reshape(n, -1, own_d)], axis=1)
    last = exchange(last.astype(BF16))
    grad_out_proj, grad_q_up, grad_kv_up = unpack_heads(heads_back, (out_proj, q_up, kv_up))
    small = jnp.sum(last[:, own_cols:].astype(F32), axis=0).reshape(-1)
    grad_down = both_halves(last[:, :own_cols], 1).reshape(-1, own_d).astype(F32)
    ffn_half = lax.optimization_barrier((ffn_half, last))[0]
    output = (hidden_one + both_halves(ffn_half, 1).astype(F32)).astype(BF16)
    edge = 2 * own_d + own_q
    edge_kv = edge + kv_gain.shape[0]
    return (
        output,
        grad_input,
        small[:own_d],
        jnp.transpose(grad_down[:qr]),
        small[2 * own_d : edge],
        grad_q_up,
        jnp.transpose(grad_down[qr:latents]),
        small[edge:edge_kv],
        grad_kv_up,
        grad_out_proj,
        small[own_d : 2 * own_d],
        jnp.transpose(small[edge_kv:].reshape(experts, own_d)),
        d_shared[0],
        d_shared[1],
        d_shared[2],
        grad_expert_gate,
        grad_expert_up,
        grad_expert_down,
    )


def solution(mesh):
    n, wt = mesh.devices.shape
    plane = math.gcd(4, n)
    mesh = jax.sharding.Mesh(
        mesh.devices.reshape(n // plane, plane, wt), CTX + ("wt",)
    )
    placed = (
        P(CTX, None),
        P(),
        P(CTX, None),
        P(CTX, None),
        P(CTX),
        P(CTX, None),
        P(CTX),
        P(CTX, "wt"),
        P(CTX, None),
        P(CTX),
        P(CTX, "wt"),
        P(CTX, "wt"),
        P(CTX),
        P(CTX, None),
        P(CTX, "wt"),
        P(CTX, "wt"),
        P(CTX, "wt"),
        P(CTX, None, "wt"),
        P(CTX, None, "wt"),
        P(CTX, "wt", None),
    )
    return jax.shard_map(
        layer,
        mesh=mesh,
        in_specs=placed,
        out_specs=(
            P(CTX, None),
            P(CTX, None),
            P(CTX),
            P(CTX, None),
            P(CTX),
            P(CTX, "wt"),
            P(CTX, None),
            P(CTX),
            P(CTX, "wt"),
            P(CTX, "wt"),
            P(CTX),
            P(CTX, None),
            P(CTX, "wt"),
            P(CTX, "wt"),
            P(CTX, "wt"),
            P(CTX, None, "wt"),
            P(CTX, None, "wt"),
            P(CTX, "wt", None),
        ),
        check_vma=False,
    )
```
